32 devices in a mesh: dp: 8 (over y, x, core), fsdp: 4 (over z).
Axes of the slice: x: 2, y: 2, z: 4, core: 2. Of those that a mesh axis runs over, the one named last changes fastest.
Arguments:
- teacher_in: bfloat16 [8, 512, 4096], P('dp', 'fsdp'), may hold values from -6 to 6
- teacher_out: bfloat16 [8, 512, 4096], P('dp', 'fsdp'), may hold values from -6 to 6
- owner_section: int32 [4], P('fsdp'), may hold values from 0 to 7
- gate_blocks: bfloat16 [32, 10, 128, 128], P('dp', None, 'fsdp'), may hold values from -0.15625 to 0.15625
- up_blocks: bfloat16 [32, 10, 128, 128], P('dp', None, 'fsdp'), may hold values from -0.15625 to 0.15625
- down_blocks: bfloat16 [32, 10, 128, 128], P('dp', None, 'fsdp'), may hold values from -0.15625 to 0.15625
- input_lists: int32 [32, 10], P('dp'), may hold values from 0 to 31, as said below
- input_counts: int32 [32], P('dp'), may hold values from 6 to 10, as said below
- output_lists: int32 [32, 10], P('dp'), may hold values from 0 to 31, as said below
- output_counts: int32 [32], P('dp'), may hold values from 6 to 10, as said below
Outputs:
- grad_gate: bfloat16 [32, 10, 128, 128], P('dp', None, 'fsdp')
- grad_up: bfloat16 [32, 10, 128, 128], P('dp', None, 'fsdp')
- grad_down: bfloat16 [32, 10, 128, 128], P('dp', None, 'fsdp')
The draws below stay inside these ranges and needn't reach their ends.
Inputs may be any that keep to these rules, and one draw needn't show every extreme that they name: `input_lists`: the first 10 entries of each row are distinct; entries at dead slots are ignored. `input_counts`: among the hidden blocks of one index of dp, one block has exactly 10 live slots. `output_lists`: the first 10 entries of each row are distinct; entries at dead slots are ignored. `output_counts`: among the hidden blocks of one index of dp, one block has exactly 10 live slots.
All inputs are finite; a program needn't handle non-finite values.
Results may differ from the reference program's by a relative error of at most 0.025.
Values may be sent and summed in bfloat16 or wider, within the bound.
No kernel may reach another device: no remote copies, remote signals or barrier semaphores. Data moves between devices by JAX's collectives and lax.ppermute only.
A program may use at most 64 MiB of HBM per device.

```python
import jax
import jax.numpy as jnp
from jax import lax

D = 4096
BLK = 128
KMAX = 10
KMIN = 6
TOK_DEV = 128
SECTIONS = 8
MICRO = 4
FF = 4096
FBLK = 32
DBLK = 32
TOKENS = 512


def block_lists(key):
    scores = jax.random.randint(key, (FBLK, DBLK), 0, 1 << 20)
    keyed = scores * DBLK + jnp.arange(DBLK, dtype=jnp.int32)[None, :]
    ordering = jnp.argsort(keyed, axis=1, stable=True)
    return ordering[:, :KMAX].astype(jnp.int32)


def block_counts(key):
    key_counts, key_forced = jax.random.split(key)
    counts = jax.random.randint(key_counts, (FBLK,), KMIN, KMAX + 1)
    per_section = FBLK // SECTIONS
    chosen = jax.random.randint(key_forced, (SECTIONS,), 0, per_section)
    forced = jnp.arange(per_section, dtype=jnp.int32)[None, :] == chosen[:, None]
    filled = jnp.where(forced, KMAX, counts.reshape(SECTIONS, per_section))
    return filled.reshape(FBLK).astype(jnp.int32)


def draw_input_lists(key, part):
    return block_lists(jax.random.fold_in(key, 11))


def draw_output_lists(key, part):
    return block_lists(jax.random.fold_in(key, 12))


def draw_input_counts(key, part):
    return block_counts(jax.random.fold_in(key, 21))


def draw_output_counts(key, part):
    return block_counts(jax.random.fold_in(key, 22))


def with_ends(result, rng, low, top_value):
    longest = result.shape.index(max(result.shape))
    spots = []
    for shift in (0, 1):
        where = [jax.random.randint(jax.random.fold_in(rng, axis), (), 0, length) for axis, length in enumerate(result.shape)]
        where[longest] = (where[longest] + shift) % result.shape[longest]
        spots.append(tuple(where))
    return result.at[spots[0]].set(low).at[spots[1]].set(top_value)


def block_scale(key, extent, cuts, smallest, high):
    def one(position, parts):
        heights = jax.random.uniform(jax.random.fold_in(jax.random.fold_in(key, 6), position), (parts,), jnp.float32, smallest / len(cuts), high / len(cuts))
        return jnp.repeat(jnp.exp(heights), extent[position] // parts).reshape((-1,) + (1,) * (len(extent) - position - 1))

    gain = one(*cuts[0])
    for cut in cuts[1:]:
        gain = gain * one(*cut)
    return gain


def bell_draw(key, extent, deviation, limit, cuts=(), kind=jnp.bfloat16):
    loudness = block_scale(key, extent, cuts, -0.22, 0.18) if cuts else 1.0
    array = jax.random.normal(key, extent, jnp.float32) * deviation * loudness
    return jnp.minimum(jnp.maximum(array, -limit), limit).astype(kind)


def setup_inputs(seed: int = 0) -> dict:
    splits = jax.random.split(jax.random.key(seed), 11)
    return {
        "teacher_in": bell_draw(splits[0], (SECTIONS, TOKENS, D), 1.0, 6.0, ((0, 8), (1, 4))),
        "teacher_out": bell_draw(splits[1], (SECTIONS, TOKENS, D), 1.0, 6.0, ((0, 8), (1, 4))),
        "owner_section": with_ends(jax.random.randint(splits[2], (MICRO,), 0, SECTIONS), jax.random.fold_in(splits[2], 1), 0, SECTIONS - 1).astype(jnp.int32),
        "gate_blocks": bell_draw(splits[3], (FBLK, KMAX, BLK, BLK), (KMAX * BLK) ** -0.5, 0.15625, ((0, 8), (2, 4))),
        "up_blocks": bell_draw(splits[4], (FBLK, KMAX, BLK, BLK), (KMAX * BLK) ** -0.5, 0.15625, ((0, 8), (2, 4))),
        "down_blocks": bell_draw(splits[5], (FBLK, KMAX, BLK, BLK), (FF * KMAX // DBLK) ** -0.5, 0.15625, ((0, 8), (2, 4))),
        "input_lists": draw_input_lists(jax.random.fold_in(splits[10], 71), 0),
        "input_counts": draw_input_counts(jax.random.fold_in(splits[10], 71), 0),
        "output_lists": draw_output_lists(jax.random.fold_in(splits[10], 71), 0),
        "output_counts": draw_output_counts(jax.random.fold_in(splits[10], 71), 0),
    }


def live_mask(counts):
    positions = jnp.arange(KMAX, dtype=jnp.int32)
    return (positions[None, :] < counts[:, None]).astype(jnp.float32)[:, :, None, None]


def reference(teacher_in, teacher_out, owner_section, gate_blocks, up_blocks, down_blocks, input_lists, input_counts, output_lists, output_counts):
    input_live = live_mask(input_counts)
    output_live = live_mask(output_counts)
    gate_live = gate_blocks.astype(jnp.float32) * input_live
    up_live = up_blocks.astype(jnp.float32) * input_live
    down_live = down_blocks.astype(jnp.float32) * output_live
    placed = (output_lists[:, :, None] == jnp.arange(DBLK, dtype=jnp.int32)[None, None, :]).astype(jnp.float32)

    def one_batch(totals, batch_index):
        root_section = owner_section[batch_index]
        row_start = batch_index * TOK_DEV
        zero_index = jnp.int32(0)
        rows_in = lax.dynamic_slice(teacher_in, (root_section, row_start, zero_index), (1, TOK_DEV, D))[0]
        rows_out = lax.dynamic_slice(teacher_out, (root_section, row_start, zero_index), (1, TOK_DEV, D))[0]
        picked = rows_in.reshape(TOK_DEV, DBLK, BLK)[:, input_lists].astype(jnp.float32)
        gate_pre = jnp.einsum("tfki,fkio->tfo", picked, gate_live)
        up_pre = jnp.einsum("tfki,fkio->tfo", picked, up_live)
        sigmoid_gate = jax.nn.sigmoid(gate_pre)
        activated = gate_pre * sigmoid_gate
        hidden = (activated * up_pre).astype(jnp.bfloat16)
        hidden_wide = hidden.astype(jnp.float32)
        pieces = jnp.einsum("tfi,fkio->tfko", hidden_wide, down_live)
        summed = jnp.einsum("tfko,fkd->tdo", pieces, placed, precision=lax.Precision.HIGHEST).reshape(TOK_DEV, D)
        scaled_error = ((summed - rows_out.astype(jnp.float32)) / MICRO).astype(jnp.bfloat16)
        error_picked = scaled_error.reshape(TOK_DEV, DBLK, BLK)[:, output_lists].astype(jnp.float32)
        down_grad = jnp.einsum("tfi,tfko->fkio", hidden_wide, error_picked) * output_live
        hidden_grad = jnp.einsum("tfko,fkio->tfi", error_picked, down_live)
        gate_error = (hidden_grad * up_pre * sigmoid_gate * (1.0 + gate_pre * (1.0 - sigmoid_gate))).astype(jnp.bfloat16)
        up_error = (hidden_grad * activated).astype(jnp.bfloat16)
        gate_grad = jnp.einsum("tfki,tfo->fkio", picked, gate_error.astype(jnp.float32)) * input_live
        up_grad = jnp.einsum("tfki,tfo->fkio", picked, up_error.astype(jnp.float32)) * input_live
        new_totals = (
            totals[0] + gate_grad.astype(jnp.bfloat16).astype(jnp.float32),
            totals[1] + up_grad.astype(jnp.bfloat16).astype(jnp.float32),
            totals[2] + down_grad.astype(jnp.bfloat16).astype(jnp.float32),
        )
        return new_totals, None

    zero_grads = (
        jnp.zeros(gate_blocks.shape, jnp.float32),
        jnp.zeros(gate_blocks.shape, jnp.float32),
        jnp.zeros(gate_blocks.shape, jnp.float32),
    )
    totals, _ = lax.scan(one_batch, zero_grads, jnp.arange(MICRO, dtype=jnp.int32))
    return (totals[0].astype(jnp.bfloat16), totals[1].astype(jnp.bfloat16), totals[2].astype(jnp.bfloat16))
```

```python
import functools

import jax
import jax.numpy as jnp
from jax import lax
from jax.experimental import pallas as pl
from jax.experimental.pallas import tpu as pltpu
from jax.sharding import PartitionSpec as P

F32 = jnp.float32
BF16 = jnp.bfloat16
VM = pl.BlockSpec(memory_space=pltpu.VMEM)
SM = pl.BlockSpec(memory_space=pltpu.SMEM)
TN = (((0,), (0,)), ((), ()))
NT = (((1,), (1,)), ((), ()))


def call(kernel, outs, scratch, name, smem, *args):
    nbytes = sum(a.size * a.dtype.itemsize for a in args) + sum(
        o.size * o.dtype.itemsize for o in outs
    )
    return pl.pallas_call(
        kernel,
        out_shape=tuple(outs),
        in_specs=[SM] * smem + [VM] * (len(args) - smem),
        out_specs=tuple(VM for _ in outs),
        scratch_shapes=scratch,
        compiler_params=pltpu.CompilerParams(vmem_limit_bytes=56 << 20),
        cost_estimate=pl.CostEstimate(flops=1 << 27, bytes_accessed=nbytes, transcendentals=0),
        name=name,
    )(*args)


def sds(shape, dtype=BF16):
    return jax.ShapeDtypeStruct(shape, dtype)


def turn_kernel(pr, tin, *outs, pieces, nb, edge):
    d = pr[0]
    half = pieces // 2
    for r in range(pieces):
        out = outs[r % 2]
        base = lax.bitwise_xor(d, r) * (nb * edge)
        for j in range(nb):
            lanes = pl.ds(pl.multiple_of(base + j * edge, edge), edge)
            out[r // 2, j * edge : (j + 1) * edge, :] = tin[:, lanes].T


def relative_block(block, d, nb):
    return lax.bitwise_xor(block // nb, d) * nb + lax.rem(block, nb)


def front_kernel(pr, lists, counts, *refs, pieces, zs, nb, rows, edge, slots, blocks):
    xs = refs[:pieces]
    gate, up = refs[pieces : pieces + 2]
    outs = refs[pieces + 2 : pieces + 2 + zs]
    gathered = refs[pieces + 2 + zs]
    xall, weights = refs[pieces + 3 + zs :]
    d = pr[0]
    tok = xs[0].shape[-1]
    for r in range(pieces):
        for s in range(zs):
            xall[r * nb * rows : (r + 1) * nb * rows, s * tok : (s + 1) * tok] = xs[r][s]
    for f in range(blocks):
        count = counts[f]
        for k in range(slots):
            b = relative_block(lists[f, k], d, nb)
            dst = slice(k * rows, (k + 1) * rows)
            gathered[f, dst, :] = xall[pl.ds(pl.multiple_of(b * rows, rows), rows), :]
            live = k < count
            weights[dst, :edge] = jnp.where(live, gate[f, k], jnp.zeros_like(gate[f, k]))
            weights[dst, edge:] = jnp.where(live, up[f, k], jnp.zeros_like(up[f, k]))
        both = lax.dot_general(gathered[f], weights[...], TN, preferred_element_type=F32)
        lanes = slice(f * edge, (f + 1) * edge)
        for s in range(zs):
            mine = both[((zs - s) % zs) * tok : ((zs - s) % zs + 1) * tok]
            outs[s][0, :, lanes] = mine[:, :edge].astype(outs[s].dtype)
            outs[s][1, :, lanes] = mine[:, edge:].astype(outs[s].dtype)


def middle_kernel(
    pr, lists, counts, *refs, pieces, zs, nb, rows, edge, slots, blocks
):
    parts = refs[:zs]
    downs = refs[zs : 2 * zs]
    tout = refs[2 * zs]
    outs = refs[2 * zs + 1 :]
    factors, hidden_out, keep, send, down_all = outs[0], outs[1 : 1 + zs], *outs[1 + zs : 4 + zs]
    acc, hidden_t = outs[4 + zs :]
    d, z, owner = pr[0], pr[1], pr[2]
    tok = tout.shape[0]
    own = owner == d
    for b in range(pieces * nb):
        term = tout[:, b * edge : (b + 1) * edge].astype(F32)
        acc[b] = jnp.where(own, -term, jnp.zeros_like(term))
    for f in range(blocks):
        count = counts[f]
        for k in range(slots):
            live = k < count
            for s in range(zs):
                at = pl.multiple_of(lax.rem(z - s + zs, zs) * rows, rows)
                block = downs[s][f, k]
                down_all[f, pl.ds(at, rows), k * edge : (k + 1) * edge] = jnp.where(
                    live, block, jnp.zeros_like(block)
                )
    for f in range(blocks):
        lanes = slice(f * edge, (f + 1) * edge)
        g = parts[0][0, :, lanes].astype(F32)
        u = parts[0][1, :, lanes].astype(F32)
        for s in range(1, zs):
            g += parts[s][0, :, lanes].astype(F32)
            u += parts[s][1, :, lanes].astype(F32)
        sig = jax.nn.sigmoid(g)
        act = g * sig
        hidden = (act * u).astype(BF16)
        factors[0, :, lanes] = (u * sig * (1.0 + g * (1.0 - sig))).astype(BF16)
        factors[1, :, lanes] = act.astype(BF16)
        hidden_t[lanes, :] = hidden.T
        prod = jnp.dot(hidden, down_all[f], preferred_element_type=F32)
        for k in range(slots):
            acc[lists[f, k]] += prod[:, k * edge : (k + 1) * edge]
        for s in range(zs):
            at = pl.multiple_of(f * edge + lax.rem(z + s, zs) * rows, rows)
            hidden_out[s][f * rows : (f + 1) * rows, :] = hidden_t[pl.ds(at, rows), :]
    for r in range(pieces):
        for j in range(nb):
            value = acc[lax.bitwise_xor(d, r) * nb + j]
            if r % 2:
                send[r // 2, j] = value.astype(BF16)
            else:
                keep[r // 2, j] = value


def back_kernel(pr, lists, *refs, pieces, nb, edge, slots, blocks):
    es = refs[:pieces]
    down_all, out, eall, ecat = refs[pieces:]
    d = pr[0]
    for r in range(pieces):
        eall[r * nb : (r + 1) * nb] = es[r][...]
    for f in range(blocks):
        for k in range(slots):
            ecat[:, k * edge : (k + 1) * edge] = eall[relative_block(lists[f, k], d, nb)]
        out[:, f * edge : (f + 1) * edge] = lax.dot_general(
            ecat[...], down_all[f], NT, preferred_element_type=F32
        ).astype(BF16)


def down_grad_kernel(pr, lists, counts, *refs, pieces, zs, nb, rows, edge, slots, blocks):
    own = refs[:pieces]
    far = refs[pieces : 2 * pieces]
    hidden = refs[2 * pieces : 2 * pieces + zs]
    out, eall, hid = refs[2 * pieces + zs :]
    d = pr[0]
    tok = hidden[0].shape[-1]
    for r in range(pieces):
        for j in range(nb):
            eall[r * nb + j, :tok, :] = own[r][j]
            for s in range(1, zs):
                eall[r * nb + j, s * tok : (s + 1) * tok, :] = far[r][s - 1, j]
    for s in range(zs):
        hid[:, s * tok : (s + 1) * tok] = hidden[s][...]
    for f in range(blocks):
        count = counts[f]
        for k in range(slots):
            grad = jnp.dot(
                hid[f * rows : (f + 1) * rows, :],
                eall[relative_block(lists[f, k], d, nb)],
                preferred_element_type=F32,
            )
            out[f, k] = jnp.where(k < count, grad, jnp.zeros_like(grad)).astype(BF16)


def up_grad_kernel(counts, *refs, zs, rows, edge, slots, blocks):
    gathered = refs[0]
    factors = refs[1 : 1 + zs]
    errors = refs[1 + zs : 1 + 2 * zs]
    gate_out, up_out, both = refs[1 + 2 * zs :]
    tok = errors[0].shape[0]
    for f in range(blocks):
        count = counts[f]
        lanes = slice(f * edge, (f + 1) * edge)
        for s in range(zs):
            dh = errors[s][:, lanes].astype(F32)
            at = slice(s * tok, (s + 1) * tok)
            both[at, :edge] = (dh * factors[s][0, :, lanes].astype(F32)).astype(BF16)
            both[at, edge:] = (dh * factors[s][1, :, lanes].astype(F32)).astype(BF16)
        grad = jnp.dot(gathered[f], both[...], preferred_element_type=F32)
        for k in range(slots):
            part = grad[k * rows : (k + 1) * rows]
            part = jnp.where(k < count, part, jnp.zeros_like(part)).astype(BF16)
            gate_out[f, k] = part[:, :edge]
            up_out[f, k] = part[:, edge:]


def broadcast(shard, axis, root):
    mine = lax.axis_index(axis) == root
    return lax.psum(jnp.where(mine, shard, jnp.zeros_like(shard)), axis)


def live_mask(counts, slot_count):
    positions = jnp.arange(slot_count, dtype=jnp.int32)
    return (positions[None, :] < counts[:, None])[:, :, None, None]


def plain_shards(
    teacher_in,
    teacher_out,
    owner_section,
    gate_blocks,
    up_blocks,
    down_blocks,
    input_lists,
    input_counts,
    output_lists,
    output_counts,
):
    root_section = owner_section[0]
    local_in = teacher_in[0]
    local_out = teacher_out[0]
    micro_count = lax.axis_size("fsdp")
    rows_in = broadcast(local_in, "dp", root_section)
    gate_full, up_full, down_full = (
        lax.all_gather(gate_blocks, "fsdp", axis=2, tiled=True),
        lax.all_gather(up_blocks, "fsdp", axis=2, tiled=True),
        lax.all_gather(down_blocks, "fsdp", axis=2, tiled=True),
    )
    slot_count = input_lists.shape[1]
    block_edge = gate_full.shape[3]
    tok_rows = rows_in.shape[0]
    model_width = rows_in.shape[1]
    row_blocks = model_width // block_edge
    input_live = live_mask(input_counts, slot_count)
    output_live = live_mask(output_counts, slot_count)
    zero_value = jnp.zeros((), jnp.bfloat16)
    gate_live = jnp.where(input_live, gate_full, zero_value)
    up_live = jnp.where(input_live, up_full, zero_value)
    down_live = jnp.where(output_live, down_full, zero_value)
    picked = rows_in.reshape(tok_rows, row_blocks, block_edge)[:, input_lists]
    gate_pre = jnp.einsum("tfki,fkio->tfo", picked, gate_live, preferred_element_type=jnp.float32)
    up_pre = jnp.einsum("tfki,fkio->tfo", picked, up_live, preferred_element_type=jnp.float32)
    sigmoid_gate = jax.nn.sigmoid(gate_pre)
    activated = gate_pre * sigmoid_gate
    hidden = (activated * up_pre).astype(jnp.bfloat16)
    pieces = jnp.einsum("tfi,fkio->tfko", hidden, down_live, preferred_element_type=jnp.float32)
    blank_out = jnp.zeros((tok_rows, row_blocks, block_edge), jnp.float32)
    partial_out = blank_out.at[:, output_lists].add(pieces).reshape(tok_rows, model_width)
    is_owner = lax.axis_index("dp") == root_section
    own_term = jnp.where(is_owner, local_out.astype(jnp.float32), jnp.float32(0.0))
    residual_rows = lax.psum((partial_out - own_term).astype(jnp.bfloat16), "dp").astype(
        jnp.float32
    )
    scaled_error = (residual_rows / micro_count).astype(jnp.bfloat16)
    error_picked = scaled_error.reshape(tok_rows, row_blocks, block_edge)[:, output_lists]
    output_scale = output_live.astype(jnp.float32)
    input_scale = input_live.astype(jnp.float32)
    down_grad = (
        jnp.einsum("tfi,tfko->fkio", hidden, error_picked, preferred_element_type=jnp.float32)
        * output_scale
    )
    hidden_grad = jnp.einsum(
        "tfko,fkio->tfi", error_picked, down_live, preferred_element_type=jnp.float32
    )
    gate_error = (
        hidden_grad * up_pre * sigmoid_gate * (1.0 + gate_pre * (1.0 - sigmoid_gate))
    ).astype(jnp.bfloat16)
    up_error = (hidden_grad * activated).astype(jnp.bfloat16)
    gate_grad = (
        jnp.einsum("tfki,tfo->fkio", picked, gate_error, preferred_element_type=jnp.float32)
        * input_scale
    )
    up_grad = (
        jnp.einsum("tfki,tfo->fkio", picked, up_error, preferred_element_type=jnp.float32)
        * input_scale
    )
    gate_sum, up_sum, down_sum = (
        lax.psum_scatter(
            gate_grad.astype(jnp.bfloat16), "fsdp", scatter_dimension=2, tiled=True
        ).astype(jnp.float32),
        lax.psum_scatter(
            up_grad.astype(jnp.bfloat16), "fsdp", scatter_dimension=2, tiled=True
        ).astype(jnp.float32),
        lax.psum_scatter(
            down_grad.astype(jnp.bfloat16), "fsdp", scatter_dimension=2, tiled=True
        ).astype(jnp.float32),
    )
    return (
        gate_sum.astype(jnp.bfloat16),
        up_sum.astype(jnp.bfloat16),
        down_sum.astype(jnp.bfloat16),
    )


def shards(
    teacher_in,
    teacher_out,
    owner_section,
    gate_blocks,
    up_blocks,
    down_blocks,
    input_lists,
    input_counts,
    output_lists,
    output_counts,
):
    pieces, zs = lax.axis_size("dp"), lax.axis_size("fsdp")
    d, z = lax.axis_index("dp"), lax.axis_index("fsdp")
    owner = owner_section[0]
    tin, tout = teacher_in[0], teacher_out[0]
    blocks, slots, rows, edge = gate_blocks.shape
    tok, width = tin.shape
    row_blocks = width // edge
    nb = row_blocks // pieces
    chips = pieces // 2
    params = jnp.stack([d, z, owner]).astype(jnp.int32)
    dims = dict(pieces=pieces, nb=nb, edge=edge)
    more = dict(zs=zs, rows=rows, slots=slots, blocks=blocks)

    def partner(a):
        return lax.ppermute(a, "dp", [(i, i ^ 1) for i in range(pieces)])

    def chip_swap(a, c):
        return lax.ppermute(a, "dp", [(i, i ^ (2 * c)) for i in range(pieces)])

    def shift(a, s):
        return lax.ppermute(a, "fsdp", [(i, (i + s) % zs) for i in range(zs)])

    def spread(a):
        per_chip = [a] + [chip_swap(a, c) for c in range(1, chips)]
        out = []
        for p in per_chip:
            out += [p, partner(p)]
        return out

    downs = [down_blocks] + [shift(down_blocks, s) for s in range(1, zs)]

    half = sds((chips, nb * edge, tok))
    kept, sent = call(
        functools.partial(turn_kernel, **dims), [half, half], [], "turn", 1, params, tin
    )
    met = partner(sent)
    is_owner = owner == d
    own_chip = lax.bitwise_xor(owner // 2, d // 2)
    piece = jnp.where(is_owner, kept[0], met[0])
    for c in range(1, chips):
        got = chip_swap(jnp.where(is_owner, kept[c], met[c]), c)
        piece = jnp.where(own_chip == c, got, piece)
    piece = piece.reshape(nb, zs, rows, tok)
    cut = [
        lax.dynamic_index_in_dim(piece, (z + s) % zs, 1, keepdims=False) for s in range(zs)
    ]
    mixed = jnp.stack([cut[0]] + [shift(cut[s], s) for s in range(1, zs)])
    xs = spread(mixed.reshape(zs, nb * rows, tok))

    part = sds((2, tok, blocks * edge))
    front = call(
        functools.partial(front_kernel, **dims, **more),
        [sds(part.shape, F32)] + [part] * (zs - 1) + [sds((blocks, slots * rows, zs * tok))],
        [pltpu.VMEM((row_blocks * rows, zs * tok), BF16), pltpu.VMEM((slots * rows, 2 * edge), BF16)],
        "front",
        3,
        params,
        input_lists,
        input_counts,
        *xs,
        gate_blocks,
        up_blocks,
    )
    gathered = front[zs]
    parts = [front[0]] + [shift(front[s], s) for s in range(1, zs)]

    middle = call(
        functools.partial(middle_kernel, **dims, **more),
        [part]
        + [sds((blocks * rows, tok))] * zs
        + [sds((chips, nb, tok, edge), F32), sds((chips, nb, tok, edge)), sds((blocks, edge, slots * edge))],
        [pltpu.VMEM((row_blocks, tok, edge), F32), pltpu.VMEM((blocks * edge, tok), BF16)],
        "middle",
        3,
        params,
        output_lists,
        output_counts,
        *parts,
        *downs,
        tout,
    )
    keep, send, down_all = middle[1 + zs :]
    factors = [middle[0]] + [shift(middle[0], s) for s in range(1, zs)]
    hidden = [middle[1]] + [shift(middle[1 + s], s) for s in range(1, zs)]

    summed = keep + partner(send).astype(F32)
    total = summed[0]
    for c in range(1, chips):
        total = total + chip_swap(summed[c].astype(BF16), c).astype(F32)
    error = (total / zs).astype(BF16)
    near = spread(error)
    far = spread(jnp.stack([shift(error, s) for s in range(1, zs)]))

    (hidden_grad,) = call(
        functools.partial(back_kernel, **dims, slots=slots, blocks=blocks),
        [sds((tok, blocks * edge))],
        [pltpu.VMEM((row_blocks, tok, edge), BF16), pltpu.VMEM((tok, slots * edge), BF16)],
        "back",
        2,
        params,
        output_lists,
        *near,
        down_all,
    )
    grads = [hidden_grad] + [shift(hidden_grad, s) for s in range(1, zs)]

    (down_grad,) = call(
        functools.partial(down_grad_kernel, **dims, **more),
        [sds(down_blocks.shape)],
        [pltpu.VMEM((row_blocks, zs * tok, edge), BF16), pltpu.VMEM((blocks * rows, zs * tok), BF16)],
        "down_grad",
        3,
        params,
        output_lists,
        output_counts,
        *near,
        *far,
        *hidden,
    )
    gate_grad, up_grad = call(
        functools.partial(up_grad_kernel, edge=edge, **more),
        [sds(gate_blocks.shape)] * 2,
        [pltpu.VMEM((zs * tok, 2 * edge), BF16)],
        "up_grad",
        1,
        input_counts,
        gathered,
        *factors,
        *grads,
    )
    return gate_grad, up_grad, down_grad


def solution(mesh):
    weights = P("dp", None, "fsdp", None)
    rows = P("dp", "fsdp", None)

    def step(*args):
        block_rows = args[3].shape[2]
        form = plain_shards if block_rows % 16 else shards
        return form(*args)

    return jax.shard_map(
        step,
        mesh=mesh,
        in_specs=(
            rows,
            rows,
            P("fsdp"),
            weights,
            weights,
            weights,
            P("dp", None),
            P("dp"),
            P("dp", None),
            P("dp"),
        ),
        out_specs=(weights, weights, weights),
        check_vma=False,
    )
```

```python
import functools

import jax
import jax.numpy as jnp
from jax import lax
from jax.experimental import pallas as pl
from jax.experimental.pallas import tpu as pltpu
from jax.sharding import PartitionSpec as P


F32 = jnp.float32
BF16 = jnp.bfloat16
VM = pl.BlockSpec(memory_space=pltpu.VMEM)
SM = pl.BlockSpec(memory_space=pltpu.SMEM)
TN = (((0,), (0,)), ((), ()))
NT = (((1,), (1,)), ((), ()))


def call(kernel, outs, scratch, smem, *args):
    nbytes = sum(a.size * a.dtype.itemsize for a in args) + sum(
        o.size * o.dtype.itemsize for o in outs
    )
    return pl.pallas_call(
        kernel,
        out_shape=tuple(outs),
        in_specs=[SM] * smem + [VM] * (len(args) - smem),
        out_specs=tuple(VM for _ in outs),
        scratch_shapes=scratch,
        compiler_params=pltpu.CompilerParams(vmem_limit_bytes=56 << 20),
        cost_estimate=pl.CostEstimate(flops=1 << 27, bytes_accessed=nbytes, transcendentals=0),
    )(*args)


def sds(shape, dtype=BF16):
    return jax.ShapeDtypeStruct(shape, dtype)


def turn_kernel(tin, *outs, pieces, nb, edge):
    d = lax.axis_index("dp")
    for r in range(pieces):
        out = outs[r % 2]
        base = lax.bitwise_xor(d, r) * (nb * edge)
        for j in range(nb):
            lanes = pl.ds(pl.multiple_of(base + j * edge, edge), edge)
            out[r // 2, j * edge : (j + 1) * edge, :] = tin[:, lanes].T


def relative_block(block, d, nb):
    return lax.bitwise_xor(block // nb, d) * nb + lax.rem(block, nb)


def front_kernel(lists, counts, *refs, pieces, zs, nb, rows, edge, slots, blocks):
    xs = refs[:pieces]
    gate, up = refs[pieces : pieces + 2]
    outs = refs[pieces + 2 : pieces + 2 + zs]
    gathered = refs[pieces + 2 + zs]
    xall, weights = refs[pieces + 3 + zs :]
    d = lax.axis_index("dp")
    tok = xs[0].shape[-1]
    for r in range(pieces):
        for s in range(zs):
            xall[r * nb * rows : (r + 1) * nb * rows, s * tok : (s + 1) * tok] = xs[r][s]
    for f in range(blocks):
        count = counts[f]
        for k in range(slots):
            b = relative_block(lists[f, k], d, nb)
            dst = slice(k * rows, (k + 1) * rows)
            gathered[f, dst, :] = xall[pl.ds(pl.multiple_of(b * rows, rows), rows), :]
            live = k < count
            weights[dst, :edge] = jnp.where(live, gate[f, k], jnp.zeros_like(gate[f, k]))
            weights[dst, edge:] = jnp.where(live, up[f, k], jnp.zeros_like(up[f, k]))
        both = lax.dot_general(gathered[f], weights[...], TN, preferred_element_type=F32)
        lanes = slice(f * edge, (f + 1) * edge)
        for s in range(zs):
            mine = both[((zs - s) % zs) * tok : ((zs - s) % zs + 1) * tok]
            outs[s][0, :, lanes] = mine[:, :edge].astype(outs[s].dtype)
            outs[s][1, :, lanes] = mine[:, edge:].astype(outs[s].dtype)


def middle_kernel(
    owners, lists, counts, *refs, pieces, zs, nb, rows, edge, slots, blocks
):
    parts = refs[:zs]
    downs = refs[zs : 2 * zs]
    tout = refs[2 * zs]
    outs = refs[2 * zs + 1 :]
    factors, hidden_out, keep, send, down_all = outs[0], outs[1 : 1 + zs], *outs[1 + zs : 4 + zs]
    acc, hidden_t = outs[4 + zs :]
    d, z, owner = lax.axis_index("dp"), lax.axis_index("fsdp"), owners[0]
    own = owner == d
    for b in range(pieces * nb):
        term = tout[:, b * edge : (b + 1) * edge].astype(F32)
        acc[b] = jnp.where(own, -term, jnp.zeros_like(term))
    for f in range(blocks):
        count = counts[f]
        for k in range(slots):
            live = k < count
            for s in range(zs):
                at = pl.multiple_of(lax.rem(z - s + zs, zs) * rows, rows)
                block = downs[s][f, k]
                down_all[f, pl.ds(at, rows), k * edge : (k + 1) * edge] = jnp.where(
                    live, block, jnp.zeros_like(block)
                )
    for f in range(blocks):
        lanes = slice(f * edge, (f + 1) * edge)
        g = parts[0][0, :, lanes].astype(F32)
        u = parts[0][1, :, lanes].astype(F32)
        for s in range(1, zs):
            g += parts[s][0, :, lanes].astype(F32)
            u += parts[s][1, :, lanes].astype(F32)
        sig = jax.nn.sigmoid(g)
        act = g * sig
        hidden = (act * u).astype(BF16)
        factors[0, :, lanes] = (u * sig * (1.0 + g * (1.0 - sig))).astype(BF16)
        factors[1, :, lanes] = act.astype(BF16)
        hidden_t[lanes, :] = hidden.T
        prod = jnp.dot(hidden, down_all[f], preferred_element_type=F32)
        for k in range(slots):
            acc[lists[f, k]] += prod[:, k * edge : (k + 1) * edge]
        for s in range(zs):
            at = pl.multiple_of(f * edge + lax.rem(z + s, zs) * rows, rows)
            hidden_out[s][f * rows : (f + 1) * rows, :] = hidden_t[pl.ds(at, rows), :]
    for r in range(pieces):
        for j in range(nb):
            value = acc[lax.bitwise_xor(d, r) * nb + j]
            if r % 2:
                send[r // 2, j] = value.astype(BF16)
            else:
                keep[r // 2, j] = value


def back_kernel(lists, *refs, pieces, nb, edge, slots, blocks):
    es = refs[:pieces]
    down_all, out, eall, ecat = refs[pieces:]
    d = lax.axis_index("dp")
    for r in range(pieces):
        eall[r * nb : (r + 1) * nb] = es[r][...]
    for f in range(blocks):
        for k in range(slots):
            ecat[:, k * edge : (k + 1) * edge] = eall[relative_block(lists[f, k], d, nb)]
        out[:, f * edge : (f + 1) * edge] = lax.dot_general(
            ecat[...], down_all[f], NT, preferred_element_type=F32
        ).astype(BF16)


def down_grad_kernel(lists, counts, *refs, pieces, zs, nb, rows, edge, slots, blocks):
    own = refs[:pieces]
    far = refs[pieces : 2 * pieces]
    hidden = refs[2 * pieces : 2 * pieces + zs]
    out, eall, hid = refs[2 * pieces + zs :]
    d = lax.axis_index("dp")
    tok = hidden[0].shape[-1]
    for r in range(pieces):
        for j in range(nb):
            eall[r * nb + j, :tok, :] = own[r][j]
            for s in range(1, zs):
                eall[r * nb + j, s * tok : (s + 1) * tok, :] = far[r][s - 1, j]
    for s in range(zs):
        hid[:, s * tok : (s + 1) * tok] = hidden[s][...]
    for f in range(blocks):
        count = counts[f]
        for k in range(slots):
            grad = jnp.dot(
                hid[f * rows : (f + 1) * rows, :],
                eall[relative_block(lists[f, k], d, nb)],
                preferred_element_type=F32,
            )
            out[f, k] = jnp.where(k < count, grad, jnp.zeros_like(grad)).astype(BF16)


def up_grad_kernel(counts, *refs, zs, rows, edge, slots, blocks):
    gathered = refs[0]
    factors = refs[1 : 1 + zs]
    errors = refs[1 + zs : 1 + 2 * zs]
    gate_out, up_out, both = refs[1 + 2 * zs :]
    tok = errors[0].shape[0]
    for f in range(blocks):
        count = counts[f]
        lanes = slice(f * edge, (f + 1) * edge)
        for s in range(zs):
            dh = errors[s][:, lanes].astype(F32)
            at = slice(s * tok, (s + 1) * tok)
            both[at, :edge] = (dh * factors[s][0, :, lanes].astype(F32)).astype(BF16)
            both[at, edge:] = (dh * factors[s][1, :, lanes].astype(F32)).astype(BF16)
        grad = jnp.dot(gathered[f], both[...], preferred_element_type=F32)
        for k in range(slots):
            part = grad[k * rows : (k + 1) * rows]
            part = jnp.where(k < count, part, jnp.zeros_like(part)).astype(BF16)
            gate_out[f, k] = part[:, :edge]
            up_out[f, k] = part[:, edge:]


def broadcast(shard, axis, root):
    mine = lax.axis_index(axis) == root
    return lax.psum(jnp.where(mine, shard, jnp.zeros_like(shard)), axis)


def live_mask(counts, slot_count):
    positions = jnp.arange(slot_count, dtype=jnp.int32)
    return (positions[None, :] < counts[:, None])[:, :, None, None]


def plain_shards(
    teacher_in,
    teacher_out,
    owner_section,
    gate_blocks,
    up_blocks,
    down_blocks,
    input_lists,
    input_counts,
    output_lists,
    output_counts,
):
    root_section = owner_section[0]
    local_in = teacher_in[0]
    local_out = teacher_out[0]
    micro_count = lax.axis_size("fsdp")
    rows_in = broadcast(local_in, "dp", root_section)
    gate_full, up_full, down_full = (
        lax.all_gather(gate_blocks, "fsdp", axis=2, tiled=True),
        lax.all_gather(up_blocks, "fsdp", axis=2, tiled=True),
        lax.all_gather(down_blocks, "fsdp", axis=2, tiled=True),
    )
    slot_count = input_lists.shape[1]
    block_edge = gate_full.shape[3]
    tok_rows = rows_in.shape[0]
    model_width = rows_in.shape[1]
    row_blocks = model_width // block_edge
    input_live = live_mask(input_counts, slot_count)
    output_live = live_mask(output_counts, slot_count)
    zero_value = jnp.zeros((), jnp.bfloat16)
    gate_live = jnp.where(input_live, gate_full, zero_value)
    up_live = jnp.where(input_live, up_full, zero_value)
    down_live = jnp.where(output_live, down_full, zero_value)
    picked = rows_in.reshape(tok_rows, row_blocks, block_edge)[:, input_lists]
    gate_pre = jnp.einsum("tfki,fkio->tfo", picked, gate_live, preferred_element_type=jnp.float32)
    up_pre = jnp.einsum("tfki,fkio->tfo", picked, up_live, preferred_element_type=jnp.float32)
    sigmoid_gate = jax.nn.sigmoid(gate_pre)
    activated = gate_pre * sigmoid_gate
    hidden = (activated * up_pre).astype(jnp.bfloat16)
    pieces = jnp.einsum("tfi,fkio->tfko", hidden, down_live, preferred_element_type=jnp.float32)
    blank_out = jnp.zeros((tok_rows, row_blocks, block_edge), jnp.float32)
    partial_out = blank_out.at[:, output_lists].add(pieces).reshape(tok_rows, model_width)
    is_owner = lax.axis_index("dp") == root_section
    own_term = jnp.where(is_owner, local_out.astype(jnp.float32), jnp.float32(0.0))
    residual_rows = lax.psum((partial_out - own_term).astype(jnp.bfloat16), "dp").astype(
        jnp.float32
    )
    scaled_error = (residual_rows / micro_count).astype(jnp.bfloat16)
    error_picked = scaled_error.reshape(tok_rows, row_blocks, block_edge)[:, output_lists]
    output_scale = output_live.astype(jnp.float32)
    input_scale = input_live.astype(jnp.float32)
    down_grad = (
        jnp.einsum("tfi,tfko->fkio", hidden, error_picked, preferred_element_type=jnp.float32)
        * output_scale
    )
    hidden_grad = jnp.einsum(
        "tfko,fkio->tfi", error_picked, down_live, preferred_element_type=jnp.float32
    )
    gate_error = (
        hidden_grad * up_pre * sigmoid_gate * (1.0 + gate_pre * (1.0 - sigmoid_gate))
    ).astype(jnp.bfloat16)
    up_error = (hidden_grad * activated).astype(jnp.bfloat16)
    gate_grad = (
        jnp.einsum("tfki,tfo->fkio", picked, gate_error, preferred_element_type=jnp.float32)
        * input_scale
    )
    up_grad = (
        jnp.einsum("tfki,tfo->fkio", picked, up_error, preferred_element_type=jnp.float32)
        * input_scale
    )
    gate_sum, up_sum, down_sum = (
        lax.psum_scatter(
            gate_grad.astype(jnp.bfloat16), "fsdp", scatter_dimension=2, tiled=True
        ).astype(jnp.float32),
        lax.psum_scatter(
            up_grad.astype(jnp.bfloat16), "fsdp", scatter_dimension=2, tiled=True
        ).astype(jnp.float32),
        lax.psum_scatter(
            down_grad.astype(jnp.bfloat16), "fsdp", scatter_dimension=2, tiled=True
        ).astype(jnp.float32),
    )
    return (
        gate_sum.astype(jnp.bfloat16),
        up_sum.astype(jnp.bfloat16),
        down_sum.astype(jnp.bfloat16),
    )


def shards(
    teacher_in,
    teacher_out,
    owner_section,
    gate_blocks,
    up_blocks,
    down_blocks,
    input_lists,
    input_counts,
    output_lists,
    output_counts,
):
    pieces, zs = lax.axis_size("dp"), lax.axis_size("fsdp")
    d, z = lax.axis_index("dp"), lax.axis_index("fsdp")
    owner = owner_section[0]
    tin, tout = teacher_in[0], teacher_out[0]
    blocks, slots, rows, edge = gate_blocks.shape
    tok, width = tin.shape
    row_blocks = width // edge
    nb = row_blocks // pieces
    chips = pieces // 2
    dims = dict(pieces=pieces, nb=nb, edge=edge)
    more = dict(zs=zs, rows=rows, slots=slots, blocks=blocks)

    def partner(a):
        return lax.ppermute(a, "dp", [(i, i ^ 1) for i in range(pieces)])

    def chip_swap(a, c):
        return lax.ppermute(a, "dp", [(i, i ^ (2 * c)) for i in range(pieces)])

    def shift(a, s):
        return lax.ppermute(a, "fsdp", [(i, (i + s) % zs) for i in range(zs)])

    def spread(a):
        per_chip = [a] + [chip_swap(a, c) for c in range(1, chips)]
        out = []
        for p in per_chip:
            out += [p, partner(p)]
        return out

    downs = [down_blocks] + [shift(down_blocks, s) for s in range(1, zs)]

    half = sds((chips, nb * edge, tok))
    kept, sent = call(functools.partial(turn_kernel, **dims), [half, half], [], 0, tin)
    met = partner(sent)
    is_owner = owner == d
    own_chip = lax.bitwise_xor(owner // 2, d // 2)
    piece = jnp.where(is_owner, kept[0], met[0])
    for c in range(1, chips):
        got = chip_swap(jnp.where(is_owner, kept[c], met[c]), c)
        piece = jnp.where(own_chip == c, got, piece)
    piece = piece.reshape(nb, zs, rows, tok)
    cut = [
        lax.dynamic_index_in_dim(piece, (z + s) % zs, 1, keepdims=False) for s in range(zs)
    ]
    mixed = jnp.stack([cut[0]] + [shift(cut[s], s) for s in range(1, zs)])
    xs = spread(mixed.reshape(zs, nb * rows, tok))

    part = sds((2, tok, blocks * edge))
    front = call(
        functools.partial(front_kernel, **dims, **more),
        [sds(part.shape, F32)] + [part] * (zs - 1) + [sds((blocks, slots * rows, zs * tok))],
        [pltpu.VMEM((row_blocks * rows, zs * tok), BF16), pltpu.VMEM((slots * rows, 2 * edge), BF16)],
        2,
        input_lists,
        input_counts,
        *xs,
        gate_blocks,
        up_blocks,
    )
    gathered = front[zs]
    parts = [front[0]] + [shift(front[s], s) for s in range(1, zs)]

    middle = call(
        functools.partial(middle_kernel, **dims, **more),
        [part]
        + [sds((blocks * rows, tok))] * zs
        + [sds((chips, nb, tok, edge), F32), sds((chips, nb, tok, edge)), sds((blocks, edge, slots * edge))],
        [pltpu.VMEM((row_blocks, tok, edge), F32), pltpu.VMEM((blocks * edge, tok), BF16)],
        3,
        owner_section,
        output_lists,
        output_counts,
        *parts,
        *downs,
        tout,
    )
    keep, send, down_all = middle[1 + zs :]
    factors = [middle[0]] + [shift(middle[0], s) for s in range(1, zs)]
    hidden = [middle[1]] + [shift(middle[1 + s], s) for s in range(1, zs)]

    summed = keep + partner(send).astype(F32)
    total = summed[0]
    for c in range(1, chips):
        total = total + chip_swap(summed[c].astype(BF16), c).astype(F32)
    error = (total / zs).astype(BF16)
    near = spread(error)
    arrived = [shift(error, s) for s in range(1, zs)]
    packed = jnp.stack(arrived)
    far = spread(packed)

    (hidden_grad,) = call(
        functools.partial(back_kernel, **dims, slots=slots, blocks=blocks),
        [sds((tok, blocks * edge))],
        [pltpu.VMEM((row_blocks, tok, edge), BF16), pltpu.VMEM((tok, slots * edge), BF16)],
        1,
        output_lists,
        *near,
        down_all,
    )
    grads = [hidden_grad] + [shift(hidden_grad, s) for s in range(1, zs)]

    (down_grad,) = call(
        functools.partial(down_grad_kernel, **dims, **more),
        [sds(down_blocks.shape)],
        [pltpu.VMEM((row_blocks, zs * tok, edge), BF16), pltpu.VMEM((blocks * rows, zs * tok), BF16)],
        2,
        output_lists,
        output_counts,
        *near,
        *far,
        *hidden,
    )
    gate_grad, up_grad = call(
        functools.partial(up_grad_kernel, edge=edge, **more),
        [sds(gate_blocks.shape)] * 2,
        [pltpu.VMEM((zs * tok, 2 * edge), BF16)],
        1,
        input_counts,
        gathered,
        *factors,
        *grads,
    )
    return gate_grad, up_grad, down_grad


def solution(mesh):
    weights = P("dp", None, "fsdp", None)
    rows = P("dp", "fsdp", None)

    def step(*args):
        block_rows = args[3].shape[2]
        if block_rows % 16:
            return plain_shards(*args)
        return shards(*args)

    return jax.shard_map(
        step,
        mesh=mesh,
        in_specs=(
            rows,
            rows,
            P("fsdp"),
            weights,
            weights,
            weights,
            P("dp", None),
            P("dp"),
            P("dp", None),
            P("dp"),
        ),
        out_specs=(weights, weights, weights),
        check_vma=False,
    )
```

```python
import functools

import jax
import jax.numpy as jnp
from jax import lax
from jax.experimental import pallas as pl
from jax.experimental.pallas import tpu as pltpu
from jax.sharding import PartitionSpec as P


F32 = jnp.float32
BF16 = jnp.bfloat16
VM = pl.BlockSpec(memory_space=pltpu.VMEM)
SM = pl.BlockSpec(memory_space=pltpu.SMEM)
TN = (((0,), (0,)), ((), ()))
NT = (((1,), (1,)), ((), ()))


def call(kernel, outs, scratch, smem, *args):
    nbytes = sum(a.size * a.dtype.itemsize for a in args) + sum(
        o.size * o.dtype.itemsize for o in outs
    )
    return pl.pallas_call(
        kernel,
        out_shape=tuple(outs),
        in_specs=[SM] * smem + [VM] * (len(args) - smem),
        out_specs=tuple(VM for _ in outs),
        scratch_shapes=scratch,
        compiler_params=pltpu.CompilerParams(vmem_limit_bytes=16 << 20),
        cost_estimate=pl.CostEstimate(flops=1 << 27, bytes_accessed=nbytes, transcendentals=0),
    )(*args)


def sds(shape, dtype=BF16):
    return jax.ShapeDtypeStruct(shape, dtype)


def far_end(z, zs):
    return jnp.logical_or(z == 0, z == zs - 1)


def turn_kernel(tin, *outs, pieces, nb, edge):
    d = lax.axis_index("dp")
    for r in range(pieces):
        out = outs[r % 2]
        base = lax.bitwise_xor(d, r) * (nb * edge)
        for j in range(nb):
            lanes = pl.ds(pl.multiple_of(base + j * edge, edge), edge)
            out[r // 2, j * edge : (j + 1) * edge, :] = tin[:, lanes].T


def relative_block(block, d, nb):
    return lax.bitwise_xor(block // nb, d) * nb + lax.rem(block, nb)


def front_kernel(lists, counts, *refs, pieces, zs, nb, rows, edge, slots, blocks):
    xs = refs[:pieces]
    gate, up = refs[pieces : pieces + 2]
    outs = refs[pieces + 2 : pieces + 2 + zs]
    gathered = refs[pieces + 2 + zs]
    xall, weights = refs[pieces + 3 + zs :]
    d = lax.axis_index("dp")
    tok = xs[0].shape[-1]
    for r in range(pieces):
        for s in range(zs):
            xall[r * nb * rows : (r + 1) * nb * rows, s * tok : (s + 1) * tok] = xs[r][s]
    for f in range(blocks):
        count = counts[f]
        for k in range(slots):
            b = relative_block(lists[f, k], d, nb)
            dst = slice(k * rows, (k + 1) * rows)
            gathered[f, dst, :] = xall[pl.ds(pl.multiple_of(b * rows, rows), rows), :]
            live = k < count
            weights[dst, :edge] = jnp.where(live, gate[f, k], jnp.zeros_like(gate[f, k]))
            weights[dst, edge:] = jnp.where(live, up[f, k], jnp.zeros_like(up[f, k]))
        both = lax.dot_general(gathered[f], weights[...], TN, preferred_element_type=F32)
        lanes = slice(f * edge, (f + 1) * edge)
        for s in range(zs):
            mine = both[s * tok : (s + 1) * tok]
            outs[s][0, :, lanes] = mine[:, :edge].astype(outs[s].dtype)
            outs[s][1, :, lanes] = mine[:, edge:].astype(outs[s].dtype)


def middle_kernel(
    owners, lists, counts, *refs, pieces, zs, nb, rows, edge, slots, blocks
):
    parts = refs[:zs]
    downs = refs[zs : 2 * zs + 1]
    tout = refs[2 * zs + 1]
    outs = refs[2 * zs + 2 :]
    factors, hidden_out, keep, send, down_all = outs[0], outs[1 : 1 + zs], *outs[1 + zs : 4 + zs]
    acc, hidden_t = outs[4 + zs :]
    d, z, owner = lax.axis_index("dp"), lax.axis_index("fsdp"), owners[0]
    own = owner == d
    for b in range(pieces * nb):
        term = tout[:, b * edge : (b + 1) * edge].astype(F32)
        acc[b] = jnp.where(own, -term, jnp.zeros_like(term))
    for f in range(blocks):
        count = counts[f]
        for k in range(slots):
            live = k < count
            for s in range(zs):
                at = pl.multiple_of(lax.bitwise_xor(z, s) * rows, rows)
                block = downs[s][f, k]
                if s == zs - 1:
                    block = jnp.where(far_end(z, zs), downs[zs][f, k], block)
                down_all[f, pl.ds(at, rows), k * edge : (k + 1) * edge] = jnp.where(
                    live, block, jnp.zeros_like(block)
                )
    for f in range(blocks):
        lanes = slice(f * edge, (f + 1) * edge)
        g = parts[0][0, :, lanes].astype(F32)
        u = parts[0][1, :, lanes].astype(F32)
        for s in range(1, zs):
            g += parts[s][0, :, lanes].astype(F32)
            u += parts[s][1, :, lanes].astype(F32)
        sig = jax.nn.sigmoid(g)
        act = g * sig
        hidden = (act * u).astype(BF16)
        factors[0, :, lanes] = (u * sig * (1.0 + g * (1.0 - sig))).astype(BF16)
        factors[1, :, lanes] = act.astype(BF16)
        hidden_t[lanes, :] = hidden.T
        prod = jnp.dot(hidden, down_all[f], preferred_element_type=F32)
        for k in range(slots):
            acc[lists[f, k]] += prod[:, k * edge : (k + 1) * edge]
        for s in range(zs):
            at = pl.multiple_of(f * edge + lax.bitwise_xor(z, s) * rows, rows)
            hidden_out[s][f * rows : (f + 1) * rows, :] = hidden_t[pl.ds(at, rows), :]
    for r in range(pieces):
        for j in range(nb):
            value = acc[lax.bitwise_xor(d, r) * nb + j]
            if r % 2:
                send[r // 2, j] = value.astype(BF16)
            else:
                keep[r // 2, j] = value


def back_kernel(lists, *refs, pieces, nb, edge, slots, blocks):
    es = refs[:pieces]
    down_all, out, eall, ecat = refs[pieces:]
    d = lax.axis_index("dp")
    for r in range(pieces):
        eall[r * nb : (r + 1) * nb] = es[r][...]
    for f in range(blocks):
        for k in range(slots):
            ecat[:, k * edge : (k + 1) * edge] = eall[relative_block(lists[f, k], d, nb)]
        out[:, f * edge : (f + 1) * edge] = lax.dot_general(
            ecat[...], down_all[f], NT, preferred_element_type=F32
        ).astype(BF16)


def down_grad_kernel(lists, counts, *refs, pieces, zs, nb, rows, edge, slots, blocks):
    own = refs[:pieces]
    far = refs[pieces : 2 * pieces]
    hidden = refs[2 * pieces : 2 * pieces + zs]
    out, eall, hid = refs[2 * pieces + zs :]
    d = lax.axis_index("dp")
    tok = hidden[0].shape[-1]
    for r in range(pieces):
        for j in range(nb):
            eall[r * nb + j, :tok, :] = own[r][j]
            for s in range(1, zs):
                eall[r * nb + j, s * tok : (s + 1) * tok, :] = far[r][s - 1, j]
    for s in range(zs):
        hid[:, s * tok : (s + 1) * tok] = hidden[s][...]
    for f in range(blocks):
        count = counts[f]
        for k in range(slots):
            grad = jnp.dot(
                hid[f * rows : (f + 1) * rows, :],
                eall[relative_block(lists[f, k], d, nb)],
                preferred_element_type=F32,
            )
            out[f, k] = jnp.where(k < count, grad, jnp.zeros_like(grad)).astype(BF16)


def up_grad_kernel(counts, *refs, zs, rows, edge, slots, blocks):
    gathered = refs[0]
    factors = refs[1 : 2 + zs]
    errors = refs[2 + zs : 2 + 2 * zs]
    gate_out, up_out, both = refs[2 + 2 * zs :]
    tok = errors[0].shape[0]
    ends = far_end(lax.axis_index("fsdp"), zs)
    for f in range(blocks):
        count = counts[f]
        lanes = slice(f * edge, (f + 1) * edge)
        for s in range(zs):
            dh = errors[s][:, lanes].astype(F32)
            at = slice(s * tok, (s + 1) * tok)
            for side in range(2):
                factor = factors[s][side, :, lanes]
                if s == zs - 1:
                    factor = jnp.where(ends, factors[zs][side, :, lanes], factor)
                both[at, side * edge : (side + 1) * edge] = (dh * factor.astype(F32)).astype(BF16)
        grad = jnp.dot(gathered[f], both[...], preferred_element_type=F32)
        for k in range(slots):
            part = grad[k * rows : (k + 1) * rows]
            part = jnp.where(k < count, part, jnp.zeros_like(part)).astype(BF16)
            gate_out[f, k] = part[:, :edge]
            up_out[f, k] = part[:, edge:]


def broadcast(shard, axis, root):
    mine = lax.axis_index(axis) == root
    return lax.psum(jnp.where(mine, shard, jnp.zeros_like(shard)), axis)


def live_mask(counts, slot_count):
    positions = jnp.arange(slot_count, dtype=jnp.int32)
    return (positions[None, :] < counts[:, None])[:, :, None, None]


def plain_shards(
    teacher_in,
    teacher_out,
    owner_section,
    gate_blocks,
    up_blocks,
    down_blocks,
    input_lists,
    input_counts,
    output_lists,
    output_counts,
):
    root_section = owner_section[0]
    local_in = teacher_in[0]
    local_out = teacher_out[0]
    micro_count = lax.axis_size("fsdp")
    rows_in = broadcast(local_in, "dp", root_section)
    gate_full, up_full, down_full = (
        lax.all_gather(gate_blocks, "fsdp", axis=2, tiled=True),
        lax.all_gather(up_blocks, "fsdp", axis=2, tiled=True),
        lax.all_gather(down_blocks, "fsdp", axis=2, tiled=True),
    )
    slot_count = input_lists.shape[1]
    block_edge = gate_full.shape[3]
    tok_rows = rows_in.shape[0]
    model_width = rows_in.shape[1]
    row_blocks = model_width // block_edge
    input_live = live_mask(input_counts, slot_count)
    output_live = live_mask(output_counts, slot_count)
    zero_value = jnp.zeros((), jnp.bfloat16)
    gate_live = jnp.where(input_live, gate_full, zero_value)
    up_live = jnp.where(input_live, up_full, zero_value)
    down_live = jnp.where(output_live, down_full, zero_value)
    picked = rows_in.reshape(tok_rows, row_blocks, block_edge)[:, input_lists]
    gate_pre = jnp.einsum("tfki,fkio->tfo", picked, gate_live, preferred_element_type=jnp.float32)
    up_pre = jnp.einsum("tfki,fkio->tfo", picked, up_live, preferred_element_type=jnp.float32)
    sigmoid_gate = jax.nn.sigmoid(gate_pre)
    activated = gate_pre * sigmoid_gate
    hidden = (activated * up_pre).astype(jnp.bfloat16)
    pieces = jnp.einsum("tfi,fkio->tfko", hidden, down_live, preferred_element_type=jnp.float32)
    blank_out = jnp.zeros((tok_rows, row_blocks, block_edge), jnp.float32)
    partial_out = blank_out.at[:, output_lists].add(pieces).reshape(tok_rows, model_width)
    is_owner = lax.axis_index("dp") == root_section
    own_term = jnp.where(is_owner, local_out.astype(jnp.float32), jnp.float32(0.0))
    residual_rows = lax.psum((partial_out - own_term).astype(jnp.bfloat16), "dp").astype(
        jnp.float32
    )
    scaled_error = (residual_rows / micro_count).astype(jnp.bfloat16)
    error_picked = scaled_error.reshape(tok_rows, row_blocks, block_edge)[:, output_lists]
    output_scale = output_live.astype(jnp.float32)
    input_scale = input_live.astype(jnp.float32)
    down_grad = (
        jnp.einsum("tfi,tfko->fkio", hidden, error_picked, preferred_element_type=jnp.float32)
        * output_scale
    )
    hidden_grad = jnp.einsum(
        "tfko,fkio->tfi", error_picked, down_live, preferred_element_type=jnp.float32
    )
    gate_error = (
        hidden_grad * up_pre * sigmoid_gate * (1.0 + gate_pre * (1.0 - sigmoid_gate))
    ).astype(jnp.bfloat16)
    up_error = (hidden_grad * activated).astype(jnp.bfloat16)
    gate_grad = (
        jnp.einsum("tfki,tfo->fkio", picked, gate_error, preferred_element_type=jnp.float32)
        * input_scale
    )
    up_grad = (
        jnp.einsum("tfki,tfo->fkio", picked, up_error, preferred_element_type=jnp.float32)
        * input_scale
    )
    gate_sum, up_sum, down_sum = (
        lax.psum_scatter(
            gate_grad.astype(jnp.bfloat16), "fsdp", scatter_dimension=2, tiled=True
        ).astype(jnp.float32),
        lax.psum_scatter(
            up_grad.astype(jnp.bfloat16), "fsdp", scatter_dimension=2, tiled=True
        ).astype(jnp.float32),
        lax.psum_scatter(
            down_grad.astype(jnp.bfloat16), "fsdp", scatter_dimension=2, tiled=True
        ).astype(jnp.float32),
    )
    return (
        gate_sum.astype(jnp.bfloat16),
        up_sum.astype(jnp.bfloat16),
        down_sum.astype(jnp.bfloat16),
    )


def shards(
    teacher_in,
    teacher_out,
    owner_section,
    gate_blocks,
    up_blocks,
    down_blocks,
    input_lists,
    input_counts,
    output_lists,
    output_counts,
):
    pieces, zs = lax.axis_size("dp"), lax.axis_size("fsdp")
    d, z = lax.axis_index("dp"), lax.axis_index("fsdp")
    owner = owner_section[0]
    tin, tout = teacher_in[0], teacher_out[0]
    blocks, slots, rows, edge = gate_blocks.shape
    tok, width = tin.shape
    row_blocks = width // edge
    nb = row_blocks // pieces
    chips = pieces // 2
    dims = dict(pieces=pieces, nb=nb, edge=edge)
    more = dict(zs=zs, rows=rows, slots=slots, blocks=blocks)

    def partner(a):
        return lax.ppermute(a, "dp", [(i, i ^ 1) for i in range(pieces)])

    def chip_swap(a, c):
        return lax.ppermute(a, "dp", [(i, i ^ (2 * c)) for i in range(pieces)])

    def shift(a, s):
        return lax.ppermute(a, "fsdp", [(i, i ^ s) for i in range(zs)])

    def gather(a):
        last = zs - 1
        out = [a] + [shift(a, s) for s in range(1, last)]
        if zs != 4:
            straight = shift(a, last)
            return out + [straight, straight]
        out.append(lax.ppermute(a, "fsdp", [(1, 2), (2, 1)]))
        out.append(lax.ppermute(out[2], "fsdp", [(1, 0), (2, 3)]))
        return out

    def spread(a):
        per_chip = [a] + [chip_swap(a, c) for c in range(1, chips)]
        out = []
        for p in per_chip:
            out += [p, partner(p)]
        return out

    downs = gather(down_blocks)

    half = sds((chips, nb * edge, tok))
    kept, sent = call(functools.partial(turn_kernel, **dims), [half, half], [], 0, tin)
    met = partner(sent)
    is_owner = owner == d
    own_chip = lax.bitwise_xor(owner // 2, d // 2)
    piece = jnp.where(is_owner, kept[0], met[0])
    for c in range(1, chips):
        got = chip_swap(jnp.where(is_owner, kept[c], met[c]), c)
        piece = jnp.where(own_chip == c, got, piece)
    piece = piece.reshape(nb, zs, rows, tok)
    cut = [
        lax.dynamic_index_in_dim(piece, lax.bitwise_xor(z, s), 1, keepdims=False)
        for s in range(zs)
    ]
    mixed = jnp.stack([cut[0]] + [shift(cut[s], s) for s in range(1, zs)])
    xs = spread(mixed.reshape(zs, nb * rows, tok))

    part = sds((2, tok, blocks * edge))
    front = call(
        functools.partial(front_kernel, **dims, **more),
        [sds(part.shape, F32)] + [part] * (zs - 1) + [sds((blocks, slots * rows, zs * tok))],
        [pltpu.VMEM((row_blocks * rows, zs * tok), BF16), pltpu.VMEM((slots * rows, 2 * edge), BF16)],
        2,
        input_lists,
        input_counts,
        *xs,
        gate_blocks,
        up_blocks,
    )
    gathered = front[zs]
    parts = [front[0]] + [shift(front[s], s) for s in range(1, zs)]

    middle = call(
        functools.partial(middle_kernel, **dims, **more),
        [part]
        + [sds((blocks * rows, tok))] * zs
        + [sds((chips, nb, tok, edge), F32), sds((chips, nb, tok, edge)), sds((blocks, edge, slots * edge))],
        [pltpu.VMEM((row_blocks, tok, edge), F32), pltpu.VMEM((blocks * edge, tok), BF16)],
        3,
        owner_section,
        output_lists,
        output_counts,
        *parts,
        *downs,
        tout,
    )
    keep, send, down_all = middle[1 + zs :]
    factors = gather(middle[0])
    hidden = [middle[1]] + [shift(middle[1 + s], s) for s in range(1, zs)]

    summed = keep + partner(send).astype(F32)
    total = summed[0]
    for c in range(1, chips):
        total = total + chip_swap(summed[c].astype(BF16), c).astype(F32)
    error = (total / zs).astype(BF16)
    near = spread(error)
    arrived = [shift(error, s) for s in range(1, zs)]
    packed = jnp.stack(arrived)
    far = spread(packed)

    (hidden_grad,) = call(
        functools.partial(back_kernel, **dims, slots=slots, blocks=blocks),
        [sds((tok, blocks * edge))],
        [pltpu.VMEM((row_blocks, tok, edge), BF16), pltpu.VMEM((tok, slots * edge), BF16)],
        1,
        output_lists,
        *near,
        down_all,
    )
    grads = [hidden_grad] + [shift(hidden_grad, s) for s in range(1, zs)]

    (down_grad,) = call(
        functools.partial(down_grad_kernel, **dims, **more),
        [sds(down_blocks.shape)],
        [pltpu.VMEM((row_blocks, zs * tok, edge), BF16), pltpu.VMEM((blocks * rows, zs * tok), BF16)],
        2,
        output_lists,
        output_counts,
        *near,
        *far,
        *hidden,
    )
    gate_grad, up_grad = call(
        functools.partial(up_grad_kernel, edge=edge, **more),
        [sds(gate_blocks.shape)] * 2,
        [pltpu.VMEM((zs * tok, 2 * edge), BF16)],
        1,
        input_counts,
        gathered,
        *factors,
        *grads,
    )
    return gate_grad, up_grad, down_grad


def solution(mesh):
    weights = P("dp", None, "fsdp", None)
    rows = P("dp", "fsdp", None)

    def step(*args):
        block_rows = args[3].shape[2]
        if block_rows % 16:
            return plain_shards(*args)
        return shards(*args)

    return jax.shard_map(
        step,
        mesh=mesh,
        in_specs=(
            rows,
            rows,
            P("fsdp"),
            weights,
            weights,
            weights,
            P("dp", None),
            P("dp"),
            P("dp", None),
            P("dp"),
        ),
        out_specs=(weights, weights, weights),
        check_vma=False,
    )
```

```python
import functools

import jax
import jax.numpy as jnp
from jax import lax
from jax.experimental import pallas as pl
from jax.experimental.pallas import tpu as pltpu
from jax.sharding import PartitionSpec as P


F32 = jnp.float32
BF16 = jnp.bfloat16
VM = pl.BlockSpec(memory_space=pltpu.VMEM)
SM = pl.BlockSpec(memory_space=pltpu.SMEM)
TN = (((0,), (0,)), ((), ()))
NT = (((1,), (1,)), ((), ()))


def call(kernel, outs, scratch, smem, *args):
    nbytes = sum(a.size * a.dtype.itemsize for a in args) + sum(
        o.size * o.dtype.itemsize for o in outs
    )
    return pl.pallas_call(
        kernel,
        out_shape=tuple(outs),
        in_specs=[SM] * smem + [VM] * (len(args) - smem),
        out_specs=tuple(VM for _ in outs),
        scratch_shapes=scratch,
        compiler_params=pltpu.CompilerParams(vmem_limit_bytes=16 << 20),
        cost_estimate=pl.CostEstimate(flops=1 << 27, bytes_accessed=nbytes, transcendentals=0),
    )(*args)


def sds(shape, dtype=BF16):
    return jax.ShapeDtypeStruct(shape, dtype)


def far_end(z, zs):
    return jnp.logical_or(z == 0, z == zs - 1)


def turn_kernel(tin, *outs, pieces, nb, edge):
    d = lax.axis_index("dp")
    for r in range(pieces):
        out = outs[r % 2]
        base = lax.bitwise_xor(d, r) * (nb * edge)
        for j in range(nb):
            lanes = pl.ds(pl.multiple_of(base + j * edge, edge), edge)
            out[r // 2, j * edge : (j + 1) * edge, :] = tin[:, lanes].T


def relative_block(block, d, nb):
    return lax.bitwise_xor(block // nb, d) * nb + lax.rem(block, nb)


def front_kernel(lists, counts, *refs, pieces, zs, nb, rows, edge, slots, blocks):
    xs = refs[:pieces]
    gate, up = refs[pieces : pieces + 2]
    outs = refs[pieces + 2 : pieces + 2 + zs]
    gathered = refs[pieces + 2 + zs]
    xall, weights = refs[pieces + 3 + zs :]
    d = lax.axis_index("dp")
    tok = xs[0].shape[-1]
    for r in range(pieces):
        for s in range(zs):
            xall[r * nb * rows : (r + 1) * nb * rows, s * tok : (s + 1) * tok] = xs[r][s]
    for f in range(blocks):
        count = counts[f]
        for k in range(slots):
            b = relative_block(lists[f, k], d, nb)
            dst = slice(k * rows, (k + 1) * rows)
            gathered[f, dst, :] = xall[pl.ds(pl.multiple_of(b * rows, rows), rows), :]
            live = k < count
            weights[dst, :edge] = jnp.where(live, gate[f, k], jnp.zeros_like(gate[f, k]))
            weights[dst, edge:] = jnp.where(live, up[f, k], jnp.zeros_like(up[f, k]))
        both = lax.dot_general(gathered[f], weights[...], TN, preferred_element_type=F32)
        lanes = slice(f * edge, (f + 1) * edge)
        for s in range(zs):
            mine = both[s * tok : (s + 1) * tok]
            outs[s][0, :, lanes] = mine[:, :edge].astype(outs[s].dtype)
            outs[s][1, :, lanes] = mine[:, edge:].astype(outs[s].dtype)


def middle_kernel(
    owners, lists, counts, *refs, pieces, zs, nb, rows, edge, slots, blocks
):
    terms = len(refs) - zs - 10
    parts = refs[:terms]
    downs = refs[terms : terms + zs + 1]
    tout = refs[terms + zs + 1]
    outs = refs[terms + zs + 2 :]
    hidden_own, plain, wide, keep, send, down_all, acc, hidden_t = outs
    d, z, owner = lax.axis_index("dp"), lax.axis_index("fsdp"), owners[0]
    tok = tout.shape[0]
    own = owner == d
    for b in range(pieces * nb):
        term = tout[:, b * edge : (b + 1) * edge].astype(F32)
        acc[b] = jnp.where(own, -term, jnp.zeros_like(term))
    for f in range(blocks):
        count = counts[f]
        for k in range(slots):
            live = k < count
            for s in range(zs):
                at = pl.multiple_of(lax.bitwise_xor(z, s) * rows, rows)
                block = downs[s][f, k]
                if s == zs - 1:
                    block = jnp.where(far_end(z, zs), downs[zs][f, k], block)
                down_all[f, pl.ds(at, rows), k * edge : (k + 1) * edge] = jnp.where(
                    live, block, jnp.zeros_like(block)
                )
    for f in range(blocks):
        lanes = slice(f * edge, (f + 1) * edge)
        g = parts[0][0, :, lanes].astype(F32)
        u = parts[0][1, :, lanes].astype(F32)
        for part in parts[1:]:
            g += part[0, :, lanes].astype(F32)
            u += part[1, :, lanes].astype(F32)
        sig = jax.nn.sigmoid(g)
        act = g * sig
        hidden = (act * u).astype(BF16)
        slope = (u * sig * (1.0 + g * (1.0 - sig))).astype(BF16)
        for message in (plain, wide):
            message[:tok, lanes] = slope
            message[tok : 2 * tok, lanes] = act.astype(BF16)
        hidden_t[lanes, :] = hidden.T
        prod = jnp.dot(hidden, down_all[f], preferred_element_type=F32)
        for k in range(slots):
            acc[lists[f, k]] += prod[:, k * edge : (k + 1) * edge]
        for s in range(zs):
            at = pl.multiple_of(f * edge + lax.bitwise_xor(z, s) * rows, rows)
            cut = hidden_t[pl.ds(at, rows), :]
            slot = slice(2 * tok + s % 2 * rows, 2 * tok + (s % 2 + 1) * rows)
            if s < 2:
                hidden_own[s, f * rows : (f + 1) * rows, :] = cut
            else:
                wide[slot, lanes] = cut
    for r in range(pieces):
        for j in range(nb):
            value = acc[lax.bitwise_xor(d, r) * nb + j]
            if r % 2:
                send[r // 2, j] = value.astype(BF16)
            else:
                keep[r // 2, j] = value


def back_kernel(lists, *refs, pieces, nb, edge, slots, blocks):
    es = refs[:pieces]
    down_all, out, eall, ecat = refs[pieces:]
    d = lax.axis_index("dp")
    for r in range(pieces):
        eall[r * nb : (r + 1) * nb] = es[r][...]
    for f in range(blocks):
        for k in range(slots):
            ecat[:, k * edge : (k + 1) * edge] = eall[relative_block(lists[f, k], d, nb)]
        out[:, f * edge : (f + 1) * edge] = lax.dot_general(
            ecat[...], down_all[f], NT, preferred_element_type=F32
        ).astype(BF16)


def down_grad_kernel(lists, counts, *refs, pieces, zs, nb, rows, edge, slots, blocks):
    own = refs[:pieces]
    far = refs[pieces : 2 * pieces]
    hidden_own, message = refs[2 * pieces : 2 * pieces + 2]
    keep, send, eall, hid = refs[2 * pieces + 2 :]
    d = lax.axis_index("dp")
    tok = hidden_own.shape[-1]
    for r in range(pieces):
        for j in range(nb):
            eall[r * nb + j, :tok, :] = own[r][j]
            eall[r * nb + j, tok:, :] = far[r][j]
    for f in range(blocks):
        lanes = slice(f * edge, (f + 1) * edge)
        for side in range(2):
            dst = slice(side * rows, (side + 1) * rows)
            hid[dst, :tok] = hidden_own[side, f * rows : (f + 1) * rows, :]
            hid[dst, tok:] = message[2 * tok + side * rows : 2 * tok + (side + 1) * rows, lanes]
        count = counts[f]
        for k in range(slots):
            grad = jnp.dot(
                hid[...],
                eall[relative_block(lists[f, k], d, nb)],
                preferred_element_type=F32,
            )
            grad = jnp.where(k < count, grad, jnp.zeros_like(grad))
            keep[f, k] = grad[:rows]
            send[f, k] = grad[rows:].astype(BF16)


def up_grad_kernel(counts, *refs, zs, rows, edge, slots, blocks):
    gathered = refs[0]
    factors = refs[1 : 2 + zs]
    errors = refs[2 + zs : 2 + 2 * zs]
    gate_out, up_out, both = refs[2 + 2 * zs :]
    tok = errors[0].shape[0]
    ends = far_end(lax.axis_index("fsdp"), zs)
    for f in range(blocks):
        count = counts[f]
        lanes = slice(f * edge, (f + 1) * edge)
        for s in range(zs):
            dh = errors[s][:, lanes].astype(F32)
            at = slice(s * tok, (s + 1) * tok)
            for side in range(2):
                span = slice(side * tok, (side + 1) * tok)
                factor = factors[s][span, lanes]
                if s == zs - 1:
                    factor = jnp.where(ends, factors[zs][span, lanes], factor)
                both[at, side * edge : (side + 1) * edge] = (dh * factor.astype(F32)).astype(BF16)
        grad = jnp.dot(gathered[f], both[...], preferred_element_type=F32)
        for k in range(slots):
            part = grad[k * rows : (k + 1) * rows]
            part = jnp.where(k < count, part, jnp.zeros_like(part)).astype(BF16)
            gate_out[f, k] = part[:, :edge]
            up_out[f, k] = part[:, edge:]


def broadcast(shard, axis, root):
    mine = lax.axis_index(axis) == root
    return lax.psum(jnp.where(mine, shard, jnp.zeros_like(shard)), axis)


def live_mask(counts, slot_count):
    positions = jnp.arange(slot_count, dtype=jnp.int32)
    return (positions[None, :] < counts[:, None])[:, :, None, None]


def plain_shards(
    teacher_in,
    teacher_out,
    owner_section,
    gate_blocks,
    up_blocks,
    down_blocks,
    input_lists,
    input_counts,
    output_lists,
    output_counts,
):
    root_section = owner_section[0]
    local_in = teacher_in[0]
    local_out = teacher_out[0]
    micro_count = lax.axis_size("fsdp")
    rows_in = broadcast(local_in, "dp", root_section)
    gate_full, up_full, down_full = (
        lax.all_gather(gate_blocks, "fsdp", axis=2, tiled=True),
        lax.all_gather(up_blocks, "fsdp", axis=2, tiled=True),
        lax.all_gather(down_blocks, "fsdp", axis=2, tiled=True),
    )
    slot_count = input_lists.shape[1]
    block_edge = gate_full.shape[3]
    tok_rows = rows_in.shape[0]
    model_width = rows_in.shape[1]
    row_blocks = model_width // block_edge
    input_live = live_mask(input_counts, slot_count)
    output_live = live_mask(output_counts, slot_count)
    zero_value = jnp.zeros((), jnp.bfloat16)
    gate_live = jnp.where(input_live, gate_full, zero_value)
    up_live = jnp.where(input_live, up_full, zero_value)
    down_live = jnp.where(output_live, down_full, zero_value)
    picked = rows_in.reshape(tok_rows, row_blocks, block_edge)[:, input_lists]
    gate_pre = jnp.einsum("tfki,fkio->tfo", picked, gate_live, preferred_element_type=jnp.float32)
    up_pre = jnp.einsum("tfki,fkio->tfo", picked, up_live, preferred_element_type=jnp.float32)
    sigmoid_gate = jax.nn.sigmoid(gate_pre)
    activated = gate_pre * sigmoid_gate
    hidden = (activated * up_pre).astype(jnp.bfloat16)
    pieces = jnp.einsum("tfi,fkio->tfko", hidden, down_live, preferred_element_type=jnp.float32)
    blank_out = jnp.zeros((tok_rows, row_blocks, block_edge), jnp.float32)
    partial_out = blank_out.at[:, output_lists].add(pieces).reshape(tok_rows, model_width)
    is_owner = lax.axis_index("dp") == root_section
    own_term = jnp.where(is_owner, local_out.astype(jnp.float32), jnp.float32(0.0))
    residual_rows = lax.psum((partial_out - own_term).astype(jnp.bfloat16), "dp").astype(
        jnp.float32
    )
    scaled_error = (residual_rows / micro_count).astype(jnp.bfloat16)
    error_picked = scaled_error.reshape(tok_rows, row_blocks, block_edge)[:, output_lists]
    output_scale = output_live.astype(jnp.float32)
    input_scale = input_live.astype(jnp.float32)
    down_grad = (
        jnp.einsum("tfi,tfko->fkio", hidden, error_picked, preferred_element_type=jnp.float32)
        * output_scale
    )
    hidden_grad = jnp.einsum(
        "tfko,fkio->tfi", error_picked, down_live, preferred_element_type=jnp.float32
    )
    gate_error = (
        hidden_grad * up_pre * sigmoid_gate * (1.0 + gate_pre * (1.0 - sigmoid_gate))
    ).astype(jnp.bfloat16)
    up_error = (hidden_grad * activated).astype(jnp.bfloat16)
    gate_grad = (
        jnp.einsum("tfki,tfo->fkio", picked, gate_error, preferred_element_type=jnp.float32)
        * input_scale
    )
    up_grad = (
        jnp.einsum("tfki,tfo->fkio", picked, up_error, preferred_element_type=jnp.float32)
        * input_scale
    )
    gate_sum, up_sum, down_sum = (
        lax.psum_scatter(
            gate_grad.astype(jnp.bfloat16), "fsdp", scatter_dimension=2, tiled=True
        ).astype(jnp.float32),
        lax.psum_scatter(
            up_grad.astype(jnp.bfloat16), "fsdp", scatter_dimension=2, tiled=True
        ).astype(jnp.float32),
        lax.psum_scatter(
            down_grad.astype(jnp.bfloat16), "fsdp", scatter_dimension=2, tiled=True
        ).astype(jnp.float32),
    )
    return (
        gate_sum.astype(jnp.bfloat16),
        up_sum.astype(jnp.bfloat16),
        down_sum.astype(jnp.bfloat16),
    )


def shards(
    teacher_in,
    teacher_out,
    owner_section,
    gate_blocks,
    up_blocks,
    down_blocks,
    input_lists,
    input_counts,
    output_lists,
    output_counts,
):
    pieces, zs = lax.axis_size("dp"), lax.axis_size("fsdp")
    d, z = lax.axis_index("dp"), lax.axis_index("fsdp")
    owner = owner_section[0]
    tin, tout = teacher_in[0], teacher_out[0]
    blocks, slots, rows, edge = gate_blocks.shape
    tok, width = tin.shape
    row_blocks = width // edge
    nb = row_blocks // pieces
    chips = pieces // 2
    dims = dict(pieces=pieces, nb=nb, edge=edge)
    more = dict(zs=zs, rows=rows, slots=slots, blocks=blocks)

    def partner(a):
        return lax.ppermute(a, "dp", [(i, i ^ 1) for i in range(pieces)])

    def chip_swap(a, c):
        return lax.ppermute(a, "dp", [(i, i ^ (2 * c)) for i in range(pieces)])

    def shift(a, s):
        return lax.ppermute(a, "fsdp", [(i, i ^ s) for i in range(zs)])

    def move(a, pairs):
        return lax.ppermute(a, "fsdp", pairs)

    def gather(plain, wide):
        side = shift(plain, 1)
        cross = shift(wide, 2)
        inner = move(plain, [(1, 2), (2, 1)])
        return [side, cross, inner, move(cross, [(1, 0), (2, 3)])]

    def collect(mine):
        joined = move(mine[3], [(0, 1), (3, 2)])
        cross = move(mine[2], [(0, 2), (3, 1)])
        inner = move(mine[3], [(1, 2), (2, 1)])
        pair = shift(mine[1], 1)
        both = (mine[2].astype(F32) + joined.astype(F32)).astype(BF16)
        return [mine[0], pair, cross, inner, move(both, [(2, 0), (1, 3)])]

    def spread(a):
        per_chip = [a] + [chip_swap(a, c) for c in range(1, chips)]
        out = []
        for p in per_chip:
            out += [p, partner(p)]
        return out

    downs = [down_blocks] + gather(down_blocks, down_blocks)

    half = sds((chips, nb * edge, tok))
    kept, sent = call(functools.partial(turn_kernel, **dims), [half, half], [], 0, tin)
    met = partner(sent)
    is_owner = owner == d
    own_chip = lax.bitwise_xor(owner // 2, d // 2)
    piece = jnp.where(is_owner, kept[0], met[0])
    for c in range(1, chips):
        got = chip_swap(jnp.where(is_owner, kept[c], met[c]), c)
        piece = jnp.where(own_chip == c, got, piece)
    piece = piece.reshape(nb, zs, rows, tok)
    cut = [
        lax.dynamic_index_in_dim(piece, lax.bitwise_xor(z, s), 1, keepdims=False)
        for s in range(zs)
    ]
    mixed = jnp.stack([cut[0]] + [shift(cut[s], s) for s in range(1, zs)])
    xs = spread(mixed.reshape(zs, nb * rows, tok))

    part = sds((2, tok, blocks * edge))
    front = call(
        functools.partial(front_kernel, **dims, **more),
        [sds(part.shape, F32)] + [part] * (zs - 1) + [sds((blocks, slots * rows, zs * tok))],
        [pltpu.VMEM((row_blocks * rows, zs * tok), BF16), pltpu.VMEM((slots * rows, 2 * edge), BF16)],
        2,
        input_lists,
        input_counts,
        *xs,
        gate_blocks,
        up_blocks,
    )
    gathered = front[zs]
    parts = collect(front[:zs])

    middle = call(
        functools.partial(middle_kernel, **dims, **more),
        [sds((2, blocks * rows, tok)), sds((2 * tok, blocks * edge))]
        + [sds((2 * tok + 2 * rows, blocks * edge))]
        + [sds((chips, nb, tok, edge), F32), sds((chips, nb, tok, edge)), sds((blocks, edge, slots * edge))],
        [pltpu.VMEM((row_blocks, tok, edge), F32), pltpu.VMEM((blocks * edge, tok), BF16)],
        3,
        owner_section,
        output_lists,
        output_counts,
        *parts,
        *downs,
        tout,
    )
    hidden_own, plain, wide, keep, send, down_all = middle
    messages = gather(plain, wide)

    summed = keep + partner(send).astype(F32)
    total = summed[0]
    for c in range(1, chips):
        total = total + chip_swap(summed[c].astype(BF16), c).astype(F32)
    error = (total / zs).astype(BF16)
    near = spread(error)
    far = spread(shift(error, 2))

    (hidden_grad,) = call(
        functools.partial(back_kernel, **dims, slots=slots, blocks=blocks),
        [sds((tok, blocks * edge))],
        [pltpu.VMEM((row_blocks, tok, edge), BF16), pltpu.VMEM((tok, slots * edge), BF16)],
        1,
        output_lists,
        *near,
        down_all,
    )
    grads = [hidden_grad] + [shift(hidden_grad, s) for s in range(1, zs)]

    kept, passed = call(
        functools.partial(down_grad_kernel, **dims, **more),
        [sds(down_blocks.shape, F32), sds(down_blocks.shape)],
        [pltpu.VMEM((row_blocks, 2 * tok, edge), BF16), pltpu.VMEM((2 * rows, 2 * tok), BF16)],
        2,
        output_lists,
        output_counts,
        *near,
        *far,
        hidden_own,
        messages[1],
    )
    down_grad = (kept + shift(passed, 1).astype(F32)).astype(BF16)
    gate_grad, up_grad = call(
        functools.partial(up_grad_kernel, edge=edge, **more),
        [sds(gate_blocks.shape)] * 2,
        [pltpu.VMEM((zs * tok, 2 * edge), BF16)],
        1,
        input_counts,
        gathered,
        plain,
        *messages,
        *grads,
    )
    return gate_grad, up_grad, down_grad


def solution(mesh):
    weights = P("dp", None, "fsdp", None)
    rows = P("dp", "fsdp", None)

    def step(*args):
        block_rows, block_edge = args[3].shape[2:]
        if mesh.shape["fsdp"] != 4 or block_rows % 16 or args[0].shape[1] != block_edge:
            return plain_shards(*args)
        return shards(*args)

    return jax.shard_map(
        step,
        mesh=mesh,
        in_specs=(
            rows,
            rows,
            P("fsdp"),
            weights,
            weights,
            weights,
            P("dp", None),
            P("dp"),
            P("dp", None),
            P("dp"),
        ),
        out_specs=(weights, weights, weights),
        check_vma=False,
    )
```

```python
import functools

import jax
import jax.numpy as jnp
from jax import lax
from jax.experimental import pallas as pl
from jax.experimental.pallas import tpu as pltpu
from jax.sharding import PartitionSpec as P


F32 = jnp.float32
BF16 = jnp.bfloat16
VM = pl.BlockSpec(memory_space=pltpu.VMEM)
SM = pl.BlockSpec(memory_space=pltpu.SMEM)
TN = (((0,), (0,)), ((), ()))
NT = (((1,), (1,)), ((), ()))


def call(kernel, outs, scratch, smem, *args):
    nbytes = sum(a.size * a.dtype.itemsize for a in args) + sum(
        o.size * o.dtype.itemsize for o in outs
    )
    return pl.pallas_call(
        kernel,
        out_shape=tuple(outs),
        in_specs=[SM] * smem + [VM] * (len(args) - smem),
        out_specs=tuple(VM for _ in outs),
        scratch_shapes=scratch,
        compiler_params=pltpu.CompilerParams(vmem_limit_bytes=16 << 20),
        cost_estimate=pl.CostEstimate(flops=1 << 27, bytes_accessed=nbytes, transcendentals=0),
    )(*args)


def sds(shape, dtype=BF16):
    return jax.ShapeDtypeStruct(shape, dtype)


def far_end(z, zs):
    return jnp.logical_or(z == 0, z == zs - 1)


def turn_kernel(tin, *outs, pieces, nb, edge):
    d = lax.axis_index("dp")
    for r in range(pieces):
        out = outs[r % 2]
        base = lax.bitwise_xor(d, r) * (nb * edge)
        for j in range(nb):
            lanes = pl.ds(pl.multiple_of(base + j * edge, edge), edge)
            out[r // 2, j * edge : (j + 1) * edge, :] = tin[:, lanes].T


def relative_block(block, d, nb):
    return lax.bitwise_xor(block // nb, d) * nb + lax.rem(block, nb)


def pair_kernel(counts, gate, up, weights, *, rows, edge, slots, blocks):
    for f in range(blocks):
        count = counts[f]
        for k in range(slots):
            dst = slice(k * rows, (k + 1) * rows)
            live = k < count
            weights[f, dst, :edge] = jnp.where(live, gate[f, k], jnp.zeros_like(gate[f, k]))
            weights[f, dst, edge:] = jnp.where(live, up[f, k], jnp.zeros_like(up[f, k]))


def join_kernel(counts, *refs, zs, rows, edge, slots, blocks):
    downs, down_all = refs[: zs + 1], refs[zs + 1]
    z = lax.axis_index("fsdp")
    ends = far_end(z, zs)
    for f in range(blocks):
        count = counts[f]
        for k in range(slots):
            live = k < count
            for s in range(zs):
                at = pl.multiple_of(lax.bitwise_xor(z, s) * rows, rows)
                block = downs[s][f, k]
                if s == zs - 1:
                    block = jnp.where(ends, downs[zs][f, k], block)
                down_all[f, pl.ds(at, rows), k * edge : (k + 1) * edge] = jnp.where(
                    live, block, jnp.zeros_like(block)
                )


def front_kernel(lists, *refs, pieces, zs, nb, rows, edge, slots, blocks):
    xs = refs[:pieces]
    weights = refs[pieces]
    outs = refs[pieces + 1 : pieces + 1 + zs]
    gathered, xall = refs[pieces + 1 + zs :]
    d = lax.axis_index("dp")
    tok = xs[0].shape[-1]
    for r in range(pieces):
        for s in range(zs):
            xall[r * nb * rows : (r + 1) * nb * rows, s * tok : (s + 1) * tok] = xs[r][s]
    for f in range(blocks):
        for k in range(slots):
            b = relative_block(lists[f, k], d, nb)
            dst = slice(k * rows, (k + 1) * rows)
            gathered[f, dst, :] = xall[pl.ds(pl.multiple_of(b * rows, rows), rows), :]
        both = lax.dot_general(gathered[f], weights[f], TN, preferred_element_type=F32)
        lanes = slice(f * edge, (f + 1) * edge)
        for s in range(zs):
            mine = both[s * tok : (s + 1) * tok]
            outs[s][0, :, lanes] = mine[:, :edge].astype(outs[s].dtype)
            outs[s][1, :, lanes] = mine[:, edge:].astype(outs[s].dtype)


def middle_kernel(
    owners, lists, *refs, pieces, zs, nb, rows, edge, slots, blocks
):
    parts = refs[:-9]
    down_all, tout, hidden_own, plain, wide, keep, send, acc, hidden_t = refs[-9:]
    d, z, owner = lax.axis_index("dp"), lax.axis_index("fsdp"), owners[0]
    tok = tout.shape[0]
    own = owner == d
    for b in range(pieces * nb):
        term = tout[:, b * edge : (b + 1) * edge].astype(F32)
        acc[b] = jnp.where(own, -term, jnp.zeros_like(term))
    for f in range(blocks):
        lanes = slice(f * edge, (f + 1) * edge)
        g = parts[0][0, :, lanes].astype(F32)
        u = parts[0][1, :, lanes].astype(F32)
        for part in parts[1:]:
            g += part[0, :, lanes].astype(F32)
            u += part[1, :, lanes].astype(F32)
        sig = jax.nn.sigmoid(g)
        act = g * sig
        hidden = (act * u).astype(BF16)
        slope = (u * sig * (1.0 + g * (1.0 - sig))).astype(BF16)
        for message in (plain, wide):
            message[:tok, lanes] = slope
            message[tok : 2 * tok, lanes] = act.astype(BF16)
        hidden_t[lanes, :] = hidden.T
        prod = jnp.dot(hidden, down_all[f], preferred_element_type=F32)
        for k in range(slots):
            acc[lists[f, k]] += prod[:, k * edge : (k + 1) * edge]
        for s in range(zs):
            at = pl.multiple_of(f * edge + lax.bitwise_xor(z, s) * rows, rows)
            cut = hidden_t[pl.ds(at, rows), :]
            slot = slice(2 * tok + s % 2 * rows, 2 * tok + (s % 2 + 1) * rows)
            if s < 2:
                hidden_own[s, f * rows : (f + 1) * rows, :] = cut
            else:
                wide[slot, lanes] = cut
    for r in range(pieces):
        for j in range(nb):
            value = acc[lax.bitwise_xor(d, r) * nb + j]
            if r % 2:
                send[r // 2, j] = value.astype(BF16)
            else:
                keep[r // 2, j] = value


def back_kernel(lists, *refs, pieces, nb, edge, slots, blocks):
    es = refs[:pieces]
    down_all, out, eall, ecat = refs[pieces:]
    d = lax.axis_index("dp")
    for r in range(pieces):
        eall[r * nb : (r + 1) * nb] = es[r][...]
    for f in range(blocks):
        for k in range(slots):
            ecat[:, k * edge : (k + 1) * edge] = eall[relative_block(lists[f, k], d, nb)]
        out[:, f * edge : (f + 1) * edge] = lax.dot_general(
            ecat[...], down_all[f], NT, preferred_element_type=F32
        ).astype(BF16)


def down_grad_kernel(lists, counts, *refs, pieces, zs, nb, rows, edge, slots, blocks):
    own = refs[:pieces]
    far = refs[pieces : 2 * pieces]
    hidden_own, message = refs[2 * pieces : 2 * pieces + 2]
    keep, send, eall, hid = refs[2 * pieces + 2 :]
    d = lax.axis_index("dp")
    tok = hidden_own.shape[-1]
    for r in range(pieces):
        for j in range(nb):
            eall[r * nb + j, :tok, :] = own[r][j]
            eall[r * nb + j, tok:, :] = far[r][j]
    for f in range(blocks):
        lanes = slice(f * edge, (f + 1) * edge)
        for side in range(2):
            dst = slice(side * rows, (side + 1) * rows)
            hid[dst, :tok] = hidden_own[side, f * rows : (f + 1) * rows, :]
            hid[dst, tok:] = message[2 * tok + side * rows : 2 * tok + (side + 1) * rows, lanes]
        count = counts[f]
        for k in range(slots):
            grad = jnp.dot(
                hid[...],
                eall[relative_block(lists[f, k], d, nb)],
                preferred_element_type=F32,
            )
            grad = jnp.where(k < count, grad, jnp.zeros_like(grad))
            keep[f, k] = grad[:rows]
            send[f, k] = grad[rows:].astype(BF16)


def up_grad_kernel(counts, *refs, zs, rows, edge, slots, blocks):
    gathered = refs[0]
    factors = refs[1 : 2 + zs]
    errors = refs[2 + zs : 2 + 2 * zs]
    gate_out, up_out, both = refs[2 + 2 * zs :]
    tok = errors[0].shape[0]
    ends = far_end(lax.axis_index("fsdp"), zs)
    for f in range(blocks):
        count = counts[f]
        lanes = slice(f * edge, (f + 1) * edge)
        for s in range(zs):
            dh = errors[s][:, lanes].astype(F32)
            at = slice(s * tok, (s + 1) * tok)
            for side in range(2):
                span = slice(side * tok, (side + 1) * tok)
                factor = factors[s][span, lanes]
                if s == zs - 1:
                    factor = jnp.where(ends, factors[zs][span, lanes], factor)
                both[at, side * edge : (side + 1) * edge] = (dh * factor.astype(F32)).astype(BF16)
        grad = jnp.dot(gathered[f], both[...], preferred_element_type=F32)
        for k in range(slots):
            part = grad[k * rows : (k + 1) * rows]
            part = jnp.where(k < count, part, jnp.zeros_like(part)).astype(BF16)
            gate_out[f, k] = part[:, :edge]
            up_out[f, k] = part[:, edge:]


def broadcast(shard, axis, root):
    mine = lax.axis_index(axis) == root
    return lax.psum(jnp.where(mine, shard, jnp.zeros_like(shard)), axis)


def live_mask(counts, slot_count):
    positions = jnp.arange(slot_count, dtype=jnp.int32)
    return (positions[None, :] < counts[:, None])[:, :, None, None]


def plain_shards(
    teacher_in,
    teacher_out,
    owner_section,
    gate_blocks,
    up_blocks,
    down_blocks,
    input_lists,
    input_counts,
    output_lists,
    output_counts,
):
    root_section = owner_section[0]
    local_in = teacher_in[0]
    local_out = teacher_out[0]
    micro_count = lax.axis_size("fsdp")
    rows_in = broadcast(local_in, "dp", root_section)
    gate_full, up_full, down_full = (
        lax.all_gather(gate_blocks, "fsdp", axis=2, tiled=True),
        lax.all_gather(up_blocks, "fsdp", axis=2, tiled=True),
        lax.all_gather(down_blocks, "fsdp", axis=2, tiled=True),
    )
    slot_count = input_lists.shape[1]
    block_edge = gate_full.shape[3]
    tok_rows = rows_in.shape[0]
    model_width = rows_in.shape[1]
    row_blocks = model_width // block_edge
    input_live = live_mask(input_counts, slot_count)
    output_live = live_mask(output_counts, slot_count)
    zero_value = jnp.zeros((), jnp.bfloat16)
    gate_live = jnp.where(input_live, gate_full, zero_value)
    up_live = jnp.where(input_live, up_full, zero_value)
    down_live = jnp.where(output_live, down_full, zero_value)
    picked = rows_in.reshape(tok_rows, row_blocks, block_edge)[:, input_lists]
    gate_pre = jnp.einsum("tfki,fkio->tfo", picked, gate_live, preferred_element_type=jnp.float32)
    up_pre = jnp.einsum("tfki,fkio->tfo", picked, up_live, preferred_element_type=jnp.float32)
    sigmoid_gate = jax.nn.sigmoid(gate_pre)
    activated = gate_pre * sigmoid_gate
    hidden = (activated * up_pre).astype(jnp.bfloat16)
    pieces = jnp.einsum("tfi,fkio->tfko", hidden, down_live, preferred_element_type=jnp.float32)
    blank_out = jnp.zeros((tok_rows, row_blocks, block_edge), jnp.float32)
    partial_out = blank_out.at[:, output_lists].add(pieces).reshape(tok_rows, model_width)
    is_owner = lax.axis_index("dp") == root_section
    own_term = jnp.where(is_owner, local_out.astype(jnp.float32), jnp.float32(0.0))
    residual_rows = lax.psum((partial_out - own_term).astype(jnp.bfloat16), "dp").astype(
        jnp.float32
    )
    scaled_error = (residual_rows / micro_count).astype(jnp.bfloat16)
    error_picked = scaled_error.reshape(tok_rows, row_blocks, block_edge)[:, output_lists]
    output_scale = output_live.astype(jnp.float32)
    input_scale = input_live.astype(jnp.float32)
    down_grad = (
        jnp.einsum("tfi,tfko->fkio", hidden, error_picked, preferred_element_type=jnp.float32)
        * output_scale
    )
    hidden_grad = jnp.einsum(
        "tfko,fkio->tfi", error_picked, down_live, preferred_element_type=jnp.float32
    )
    gate_error = (
        hidden_grad * up_pre * sigmoid_gate * (1.0 + gate_pre * (1.0 - sigmoid_gate))
    ).astype(jnp.bfloat16)
    up_error = (hidden_grad * activated).astype(jnp.bfloat16)
    gate_grad = (
        jnp.einsum("tfki,tfo->fkio", picked, gate_error, preferred_element_type=jnp.float32)
        * input_scale
    )
    up_grad = (
        jnp.einsum("tfki,tfo->fkio", picked, up_error, preferred_element_type=jnp.float32)
        * input_scale
    )
    gate_sum, up_sum, down_sum = (
        lax.psum_scatter(
            gate_grad.astype(jnp.bfloat16), "fsdp", scatter_dimension=2, tiled=True
        ).astype(jnp.float32),
        lax.psum_scatter(
            up_grad.astype(jnp.bfloat16), "fsdp", scatter_dimension=2, tiled=True
        ).astype(jnp.float32),
        lax.psum_scatter(
            down_grad.astype(jnp.bfloat16), "fsdp", scatter_dimension=2, tiled=True
        ).astype(jnp.float32),
    )
    return (
        gate_sum.astype(jnp.bfloat16),
        up_sum.astype(jnp.bfloat16),
        down_sum.astype(jnp.bfloat16),
    )


def shards(
    teacher_in,
    teacher_out,
    owner_section,
    gate_blocks,
    up_blocks,
    down_blocks,
    input_lists,
    input_counts,
    output_lists,
    output_counts,
):
    pieces, zs = lax.axis_size("dp"), lax.axis_size("fsdp")
    d, z = lax.axis_index("dp"), lax.axis_index("fsdp")
    owner = owner_section[0]
    tin, tout = teacher_in[0], teacher_out[0]
    blocks, slots, rows, edge = gate_blocks.shape
    tok, width = tin.shape
    row_blocks = width // edge
    nb = row_blocks // pieces
    chips = pieces // 2
    dims = dict(pieces=pieces, nb=nb, edge=edge)
    more = dict(zs=zs, rows=rows, slots=slots, blocks=blocks)

    def partner(a):
        return lax.ppermute(a, "dp", [(i, i ^ 1) for i in range(pieces)])

    def chip_swap(a, c):
        return lax.ppermute(a, "dp", [(i, i ^ (2 * c)) for i in range(pieces)])

    def shift(a, s):
        return lax.ppermute(a, "fsdp", [(i, i ^ s) for i in range(zs)])

    def move(a, pairs):
        return lax.ppermute(a, "fsdp", pairs)

    def gather(plain, wide):
        side = shift(plain, 1)
        cross = shift(wide, 2)
        inner = move(plain, [(1, 2), (2, 1)])
        core = cross[: plain.shape[0]]
        return [side, cross, inner, move(core, [(1, 0), (2, 3)])]

    def collect(mine):
        joined = move(mine[3], [(0, 1), (3, 2)])
        cross = move(mine[2], [(0, 2), (3, 1)])
        inner = move(mine[3], [(1, 2), (2, 1)])
        pair = shift(mine[1], 1)
        both = (mine[2].astype(F32) + joined.astype(F32)).astype(BF16)
        return [mine[0], pair, cross, inner, move(both, [(2, 0), (1, 3)])]

    def spread(a):
        per_chip = [a] + [chip_swap(a, c) for c in range(1, chips)]
        out = []
        for p in per_chip:
            out += [p, partner(p)]
        return out

    downs = [down_blocks] + gather(down_blocks, down_blocks)

    half = sds((chips, nb * edge, tok))
    kept, sent = call(functools.partial(turn_kernel, **dims), [half, half], [], 0, tin)
    met = partner(sent)
    is_owner = owner == d
    own_chip = lax.bitwise_xor(owner // 2, d // 2)
    piece = jnp.where(is_owner, kept[0], met[0])
    for c in range(1, chips):
        got = chip_swap(jnp.where(is_owner, kept[c], met[c]), c)
        piece = jnp.where(own_chip == c, got, piece)
    piece = piece.reshape(nb, zs, rows, tok)
    cut = [
        lax.dynamic_index_in_dim(piece, lax.bitwise_xor(z, s), 1, keepdims=False)
        for s in range(zs)
    ]
    mixed = jnp.stack([cut[0]] + [shift(cut[s], s) for s in range(1, zs)])
    xs = spread(mixed.reshape(zs, nb * rows, tok))

    part = sds((2, tok, blocks * edge))
    inner_sizes = dict(rows=rows, edge=edge, slots=slots, blocks=blocks)
    (weights,) = call(
        functools.partial(pair_kernel, **inner_sizes),
        [sds((blocks, slots * rows, 2 * edge))],
        [],
        1,
        input_counts,
        gate_blocks,
        up_blocks,
    )
    front = call(
        functools.partial(front_kernel, **dims, **more),
        [sds(part.shape, F32)] + [part] * (zs - 1) + [sds((blocks, slots * rows, zs * tok))],
        [pltpu.VMEM((row_blocks * rows, zs * tok), BF16)],
        1,
        input_lists,
        *xs,
        weights,
    )
    gathered = front[zs]
    parts = collect(front[:zs])

    (down_all,) = call(
        functools.partial(join_kernel, zs=zs, **inner_sizes),
        [sds((blocks, edge, slots * edge))],
        [],
        1,
        output_counts,
        *downs,
    )
    hidden_own, plain, wide, keep, send = call(
        functools.partial(middle_kernel, **dims, **more),
        [sds((2, blocks * rows, tok)), sds((2 * tok, blocks * edge))]
        + [sds((2 * tok + 2 * rows, blocks * edge))]
        + [sds((chips, nb, tok, edge), F32), sds((chips, nb, tok, edge))],
        [pltpu.VMEM((row_blocks, tok, edge), F32), pltpu.VMEM((blocks * edge, tok), BF16)],
        2,
        owner_section,
        output_lists,
        *parts,
        down_all,
        tout,
    )
    messages = gather(plain, wide)

    summed = keep + partner(send).astype(F32)
    total = summed[0]
    for c in range(1, chips):
        total = total + chip_swap(summed[c].astype(BF16), c).astype(F32)
    error = (total / zs).astype(BF16)
    near = spread(error)
    far = spread(shift(error, 2))

    (hidden_grad,) = call(
        functools.partial(back_kernel, **dims, slots=slots, blocks=blocks),
        [sds((tok, blocks * edge))],
        [pltpu.VMEM((row_blocks, tok, edge), BF16), pltpu.VMEM((tok, slots * edge), BF16)],
        1,
        output_lists,
        *near,
        down_all,
    )
    grads = [hidden_grad] + [shift(hidden_grad, s) for s in range(1, zs)]

    kept, passed = call(
        functools.partial(down_grad_kernel, **dims, **more),
        [sds(down_blocks.shape, F32), sds(down_blocks.shape)],
        [pltpu.VMEM((row_blocks, 2 * tok, edge), BF16), pltpu.VMEM((2 * rows, 2 * tok), BF16)],
        2,
        output_lists,
        output_counts,
        *near,
        *far,
        hidden_own,
        messages[1],
    )
    down_grad = (kept + shift(passed, 1).astype(F32)).astype(BF16)
    gate_grad, up_grad = call(
        functools.partial(up_grad_kernel, edge=edge, **more),
        [sds(gate_blocks.shape)] * 2,
        [pltpu.VMEM((zs * tok, 2 * edge), BF16)],
        1,
        input_counts,
        gathered,
        plain,
        *messages,
        *grads,
    )
    return gate_grad, up_grad, down_grad


def solution(mesh):
    weights = P("dp", None, "fsdp", None)
    rows = P("dp", "fsdp", None)

    def step(*args):
        block_rows, block_edge = args[3].shape[2:]
        if mesh.shape["fsdp"] != 4 or block_rows % 16 or args[0].shape[1] != block_edge:
            return plain_shards(*args)
        return shards(*args)

    return jax.shard_map(
        step,
        mesh=mesh,
        in_specs=(
            rows,
            rows,
            P("fsdp"),
            weights,
            weights,
            weights,
            P("dp", None),
            P("dp"),
            P("dp", None),
            P("dp"),
        ),
        out_specs=(weights, weights, weights),
        check_vma=False,
    )
```

```python
import functools

import jax
import jax.numpy as jnp
from jax import lax
from jax.experimental import pallas as pl
from jax.experimental.pallas import tpu as pltpu
from jax.sharding import PartitionSpec as P


F32 = jnp.float32
BF16 = jnp.bfloat16
VM = pl.BlockSpec(memory_space=pltpu.VMEM)
SM = pl.BlockSpec(memory_space=pltpu.SMEM)
TN = (((0,), (0,)), ((), ()))
NT = (((1,), (1,)), ((), ()))


def call(kernel, outs, scratch, smem, *args):
    nbytes = sum(a.size * a.dtype.itemsize for a in args) + sum(
        o.size * o.dtype.itemsize for o in outs
    )
    return pl.pallas_call(
        kernel,
        out_shape=tuple(outs),
        in_specs=[SM] * smem + [VM] * (len(args) - smem),
        out_specs=tuple(VM for _ in outs),
        scratch_shapes=scratch,
        compiler_params=pltpu.CompilerParams(vmem_limit_bytes=16 << 20),
        cost_estimate=pl.CostEstimate(flops=1 << 27, bytes_accessed=nbytes, transcendentals=0),
    )(*args)


def sds(shape, dtype=BF16):
    return jax.ShapeDtypeStruct(shape, dtype)


def far_end(z, zs):
    return jnp.logical_or(z == 0, z == zs - 1)


def turn_kernel(tin, *outs, pieces, nb, edge):
    d = lax.axis_index("dp")
    for r in range(pieces):
        out = outs[r % 2]
        base = lax.bitwise_xor(d, r) * (nb * edge)
        for j in range(nb):
            lanes = pl.ds(pl.multiple_of(base + j * edge, edge), edge)
            out[r // 2, j * edge : (j + 1) * edge, :] = tin[:, lanes].T


def relative_block(block, d, nb):
    return lax.bitwise_xor(block // nb, d) * nb + lax.rem(block, nb)


def pair_kernel(counts, gate, up, weights, *, rows, edge, slots, blocks):
    for f in range(blocks):
        count = counts[f]
        for k in range(slots):
            dst = slice(k * rows, (k + 1) * rows)
            live = k < count
            weights[f, dst, :edge] = jnp.where(live, gate[f, k], jnp.zeros_like(gate[f, k]))
            weights[f, dst, edge:] = jnp.where(live, up[f, k], jnp.zeros_like(up[f, k]))


def join_kernel(counts, *refs, zs, rows, edge, slots, blocks):
    downs, down_all = refs[: zs + 1], refs[zs + 1]
    z = lax.axis_index("fsdp")
    ends = far_end(z, zs)
    for f in range(blocks):
        count = counts[f]
        for k in range(slots):
            live = k < count
            for s in range(zs):
                at = pl.multiple_of(lax.bitwise_xor(z, s) * rows, rows)
                block = downs[s][f, k]
                if s == zs - 1:
                    block = jnp.where(ends, downs[zs][f, k], block)
                down_all[f, pl.ds(at, rows), k * edge : (k + 1) * edge] = jnp.where(
                    live, block, jnp.zeros_like(block)
                )


def partials(gathered, weights, outs, numbers, tok, edge, blocks):
    for f in range(blocks):
        lanes = slice(f * edge, (f + 1) * edge)
        for s, out in zip(numbers, outs):
            both = lax.dot_general(
                gathered[f, :, s * tok : (s + 1) * tok],
                weights[f],
                TN,
                preferred_element_type=F32,
            )
            out[0, :, lanes] = both[:, :edge].astype(out.dtype)
            out[1, :, lanes] = both[:, edge:].astype(out.dtype)


def front_kernel(lists, *refs, pieces, zs, nb, rows, edge, slots, blocks):
    xs = refs[:pieces]
    weights, last, gathered, xall = refs[pieces:]
    d = lax.axis_index("dp")
    tok = xs[0].shape[-1]
    for r in range(pieces):
        for s in range(zs):
            xall[r * nb * rows : (r + 1) * nb * rows, s * tok : (s + 1) * tok] = xs[r][s]
    for f in range(blocks):
        for k in range(slots):
            b = relative_block(lists[f, k], d, nb)
            dst = slice(k * rows, (k + 1) * rows)
            gathered[f, dst, :] = xall[pl.ds(pl.multiple_of(b * rows, rows), rows), :]
    partials(gathered, weights, [last], [zs - 1], tok, edge, blocks)


def rest_kernel(gathered, weights, *outs, edge, blocks):
    numbers = list(range(len(outs)))
    partials(gathered, weights, outs, numbers, outs[0].shape[1], edge, blocks)


def middle_kernel(
    owners, lists, *refs, pieces, zs, nb, rows, edge, slots, blocks
):
    parts = refs[:-9]
    down_all, tout, hidden_own, plain, wide, keep, send, acc, hidden_t = refs[-9:]
    d, z, owner = lax.axis_index("dp"), lax.axis_index("fsdp"), owners[0]
    tok = tout.shape[0]
    own = owner == d
    for b in range(pieces * nb):
        term = tout[:, b * edge : (b + 1) * edge].astype(F32)
        acc[b] = jnp.where(own, -term, jnp.zeros_like(term))
    for f in range(blocks):
        lanes = slice(f * edge, (f + 1) * edge)
        g = parts[0][0, :, lanes].astype(F32)
        u = parts[0][1, :, lanes].astype(F32)
        for part in parts[1:]:
            g += part[0, :, lanes].astype(F32)
            u += part[1, :, lanes].astype(F32)
        sig = jax.nn.sigmoid(g)
        act = g * sig
        hidden = (act * u).astype(BF16)
        slope = (u * sig * (1.0 + g * (1.0 - sig))).astype(BF16)
        for message in (plain, wide):
            message[:tok, lanes] = slope
            message[tok : 2 * tok, lanes] = act.astype(BF16)
        hidden_t[lanes, :] = hidden.T
        prod = jnp.dot(hidden, down_all[f], preferred_element_type=F32)
        for k in range(slots):
            acc[lists[f, k]] += prod[:, k * edge : (k + 1) * edge]
        for s in range(zs):
            at = pl.multiple_of(f * edge + lax.bitwise_xor(z, s) * rows, rows)
            cut = hidden_t[pl.ds(at, rows), :]
            slot = slice(2 * tok + s % 2 * rows, 2 * tok + (s % 2 + 1) * rows)
            if s < 2:
                hidden_own[s, f * rows : (f + 1) * rows, :] = cut
            else:
                wide[slot, lanes] = cut
    for r in range(pieces):
        for j in range(nb):
            value = acc[lax.bitwise_xor(d, r) * nb + j]
            if r % 2:
                send[r // 2, j] = value.astype(BF16)
            else:
                keep[r // 2, j] = value


def back_kernel(lists, *refs, pieces, nb, edge, slots, blocks):
    es = refs[:pieces]
    down_all, out, eall, ecat = refs[pieces:]
    d = lax.axis_index("dp")
    for r in range(pieces):
        eall[r * nb : (r + 1) * nb] = es[r][...]
    for f in range(blocks):
        for k in range(slots):
            ecat[:, k * edge : (k + 1) * edge] = eall[relative_block(lists[f, k], d, nb)]
        out[:, f * edge : (f + 1) * edge] = lax.dot_general(
            ecat[...], down_all[f], NT, preferred_element_type=F32
        ).astype(BF16)


def down_grad_kernel(lists, counts, *refs, pieces, zs, nb, rows, edge, slots, blocks):
    own = refs[:pieces]
    far = refs[pieces : 2 * pieces]
    hidden_own, message = refs[2 * pieces : 2 * pieces + 2]
    keep, send, eall, hid = refs[2 * pieces + 2 :]
    d = lax.axis_index("dp")
    tok = hidden_own.shape[-1]
    for r in range(pieces):
        for j in range(nb):
            eall[r * nb + j, :tok, :] = own[r][j]
            eall[r * nb + j, tok:, :] = far[r][j]
    for f in range(blocks):
        lanes = slice(f * edge, (f + 1) * edge)
        for side in range(2):
            dst = slice(side * rows, (side + 1) * rows)
            hid[dst, :tok] = hidden_own[side, f * rows : (f + 1) * rows, :]
            hid[dst, tok:] = message[2 * tok + side * rows : 2 * tok + (side + 1) * rows, lanes]
        count = counts[f]
        for k in range(slots):
            grad = jnp.dot(
                hid[...],
                eall[relative_block(lists[f, k], d, nb)],
                preferred_element_type=F32,
            )
            grad = jnp.where(k < count, grad, jnp.zeros_like(grad))
            keep[f, k] = grad[:rows]
            send[f, k] = grad[rows:].astype(BF16)


def up_grad_kernel(counts, *refs, zs, rows, edge, slots, blocks):
    gathered = refs[0]
    factors = refs[1 : 2 + zs]
    errors = refs[2 + zs : 2 + 2 * zs]
    gate_out, up_out, both = refs[2 + 2 * zs :]
    tok = errors[0].shape[0]
    ends = far_end(lax.axis_index("fsdp"), zs)
    for f in range(blocks):
        count = counts[f]
        lanes = slice(f * edge, (f + 1) * edge)
        for s in range(zs):
            dh = errors[s][:, lanes].astype(F32)
            at = slice(s * tok, (s + 1) * tok)
            for side in range(2):
                span = slice(side * tok, (side + 1) * tok)
                factor = factors[s][span, lanes]
                if s == zs - 1:
                    factor = jnp.where(ends, factors[zs][span, lanes], factor)
                both[at, side * edge : (side + 1) * edge] = (dh * factor.astype(F32)).astype(BF16)
        grad = jnp.dot(gathered[f], both[...], preferred_element_type=F32)
        for k in range(slots):
            part = grad[k * rows : (k + 1) * rows]
            part = jnp.where(k < count, part, jnp.zeros_like(part)).astype(BF16)
            gate_out[f, k] = part[:, :edge]
            up_out[f, k] = part[:, edge:]


def broadcast(shard, axis, root):
    mine = lax.axis_index(axis) == root
    return lax.psum(jnp.where(mine, shard, jnp.zeros_like(shard)), axis)


def live_mask(counts, slot_count):
    positions = jnp.arange(slot_count, dtype=jnp.int32)
    return (positions[None, :] < counts[:, None])[:, :, None, None]


def plain_shards(
    teacher_in,
    teacher_out,
    owner_section,
    gate_blocks,
    up_blocks,
    down_blocks,
    input_lists,
    input_counts,
    output_lists,
    output_counts,
):
    root_section = owner_section[0]
    local_in = teacher_in[0]
    local_out = teacher_out[0]
    micro_count = lax.axis_size("fsdp")
    rows_in = broadcast(local_in, "dp", root_section)
    gate_full, up_full, down_full = (
        lax.all_gather(gate_blocks, "fsdp", axis=2, tiled=True),
        lax.all_gather(up_blocks, "fsdp", axis=2, tiled=True),
        lax.all_gather(down_blocks, "fsdp", axis=2, tiled=True),
    )
    slot_count = input_lists.shape[1]
    block_edge = gate_full.shape[3]
    tok_rows = rows_in.shape[0]
    model_width = rows_in.shape[1]
    row_blocks = model_width // block_edge
    input_live = live_mask(input_counts, slot_count)
    output_live = live_mask(output_counts, slot_count)
    zero_value = jnp.zeros((), jnp.bfloat16)
    gate_live = jnp.where(input_live, gate_full, zero_value)
    up_live = jnp.where(input_live, up_full, zero_value)
    down_live = jnp.where(output_live, down_full, zero_value)
    picked = rows_in.reshape(tok_rows, row_blocks, block_edge)[:, input_lists]
    gate_pre = jnp.einsum("tfki,fkio->tfo", picked, gate_live, preferred_element_type=jnp.float32)
    up_pre = jnp.einsum("tfki,fkio->tfo", picked, up_live, preferred_element_type=jnp.float32)
    sigmoid_gate = jax.nn.sigmoid(gate_pre)
    activated = gate_pre * sigmoid_gate
    hidden = (activated * up_pre).astype(jnp.bfloat16)
    pieces = jnp.einsum("tfi,fkio->tfko", hidden, down_live, preferred_element_type=jnp.float32)
    blank_out = jnp.zeros((tok_rows, row_blocks, block_edge), jnp.float32)
    partial_out = blank_out.at[:, output_lists].add(pieces).reshape(tok_rows, model_width)
    is_owner = lax.axis_index("dp") == root_section
    own_term = jnp.where(is_owner, local_out.astype(jnp.float32), jnp.float32(0.0))
    residual_rows = lax.psum((partial_out - own_term).astype(jnp.bfloat16), "dp").astype(
        jnp.float32
    )
    scaled_error = (residual_rows / micro_count).astype(jnp.bfloat16)
    error_picked = scaled_error.reshape(tok_rows, row_blocks, block_edge)[:, output_lists]
    output_scale = output_live.astype(jnp.float32)
    input_scale = input_live.astype(jnp.float32)
    down_grad = (
        jnp.einsum("tfi,tfko->fkio", hidden, error_picked, preferred_element_type=jnp.float32)
        * output_scale
    )
    hidden_grad = jnp.einsum(
        "tfko,fkio->tfi", error_picked, down_live, preferred_element_type=jnp.float32
    )
    gate_error = (
        hidden_grad * up_pre * sigmoid_gate * (1.0 + gate_pre * (1.0 - sigmoid_gate))
    ).astype(jnp.bfloat16)
    up_error = (hidden_grad * activated).astype(jnp.bfloat16)
    gate_grad = (
        jnp.einsum("tfki,tfo->fkio", picked, gate_error, preferred_element_type=jnp.float32)
        * input_scale
    )
    up_grad = (
        jnp.einsum("tfki,tfo->fkio", picked, up_error, preferred_element_type=jnp.float32)
        * input_scale
    )
    gate_sum, up_sum, down_sum = (
        lax.psum_scatter(
            gate_grad.astype(jnp.bfloat16), "fsdp", scatter_dimension=2, tiled=True
        ).astype(jnp.float32),
        lax.psum_scatter(
            up_grad.astype(jnp.bfloat16), "fsdp", scatter_dimension=2, tiled=True
        ).astype(jnp.float32),
        lax.psum_scatter(
            down_grad.astype(jnp.bfloat16), "fsdp", scatter_dimension=2, tiled=True
        ).astype(jnp.float32),
    )
    return (
        gate_sum.astype(jnp.bfloat16),
        up_sum.astype(jnp.bfloat16),
        down_sum.astype(jnp.bfloat16),
    )


def shards(
    teacher_in,
    teacher_out,
    owner_section,
    gate_blocks,
    up_blocks,
    down_blocks,
    input_lists,
    input_counts,
    output_lists,
    output_counts,
):
    pieces, zs = lax.axis_size("dp"), lax.axis_size("fsdp")
    d, z = lax.axis_index("dp"), lax.axis_index("fsdp")
    owner = owner_section[0]
    tin, tout = teacher_in[0], teacher_out[0]
    blocks, slots, rows, edge = gate_blocks.shape
    tok, width = tin.shape
    row_blocks = width // edge
    nb = row_blocks // pieces
    chips = pieces // 2
    dims = dict(pieces=pieces, nb=nb, edge=edge)
    more = dict(zs=zs, rows=rows, slots=slots, blocks=blocks)

    def partner(a):
        return lax.ppermute(a, "dp", [(i, i ^ 1) for i in range(pieces)])

    def chip_swap(a, c):
        return lax.ppermute(a, "dp", [(i, i ^ (2 * c)) for i in range(pieces)])

    def shift(a, s):
        return lax.ppermute(a, "fsdp", [(i, i ^ s) for i in range(zs)])

    def move(a, pairs):
        return lax.ppermute(a, "fsdp", pairs)

    def gather(plain, wide):
        side = shift(plain, 1)
        cross = shift(wide, 2)
        inner = move(plain, [(1, 2), (2, 1)])
        core = cross[: plain.shape[0]]
        return [side, cross, inner, move(core, [(1, 0), (2, 3)])]

    def collect(mine):
        joined = move(mine[3], [(0, 1), (3, 2)])
        cross = move(mine[2], [(0, 2), (3, 1)])
        inner = move(mine[3], [(1, 2), (2, 1)])
        pair = shift(mine[1], 1)
        both = (mine[2].astype(F32) + joined.astype(F32)).astype(BF16)
        return [mine[0], pair, cross, inner, move(both, [(2, 0), (1, 3)])]

    def spread(a):
        per_chip = [a] + [chip_swap(a, c) for c in range(1, chips)]
        out = []
        for p in per_chip:
            out += [p, partner(p)]
        return out

    downs = [down_blocks] + gather(down_blocks, down_blocks)

    half = sds((chips, nb * edge, tok))
    kept, sent = call(functools.partial(turn_kernel, **dims), [half, half], [], 0, tin)
    met = partner(sent)
    is_owner = owner == d
    own_chip = lax.bitwise_xor(owner // 2, d // 2)
    piece = jnp.where(is_owner, kept[0], met[0])
    for c in range(1, chips):
        got = chip_swap(jnp.where(is_owner, kept[c], met[c]), c)
        piece = jnp.where(own_chip == c, got, piece)
    piece = piece.reshape(nb, zs, rows, tok)
    cut = [
        lax.dynamic_index_in_dim(piece, lax.bitwise_xor(z, s), 1, keepdims=False)
        for s in range(zs)
    ]
    mixed = jnp.stack([cut[0]] + [shift(cut[s], s) for s in range(1, zs)])
    xs = spread(mixed.reshape(zs, nb * rows, tok))

    part = sds((2, tok, blocks * edge))
    inner_sizes = dict(rows=rows, edge=edge, slots=slots, blocks=blocks)
    (weights,) = call(
        functools.partial(pair_kernel, **inner_sizes),
        [sds((blocks, slots * rows, 2 * edge))],
        [],
        1,
        input_counts,
        gate_blocks,
        up_blocks,
    )
    last, gathered = call(
        functools.partial(front_kernel, **dims, **more),
        [part, sds((blocks, slots * rows, zs * tok))],
        [pltpu.VMEM((row_blocks * rows, zs * tok), BF16)],
        1,
        input_lists,
        *xs,
        weights,
    )
    rest = call(
        functools.partial(rest_kernel, edge=edge, blocks=blocks),
        [sds(part.shape, F32)] + [part] * (zs - 2),
        [],
        0,
        gathered,
        weights,
    )
    parts = collect([*rest, last])

    (down_all,) = call(
        functools.partial(join_kernel, zs=zs, **inner_sizes),
        [sds((blocks, edge, slots * edge))],
        [],
        1,
        output_counts,
        *downs,
    )
    hidden_own, plain, wide, keep, send = call(
        functools.partial(middle_kernel, **dims, **more),
        [sds((2, blocks * rows, tok)), sds((2 * tok, blocks * edge))]
        + [sds((2 * tok + 2 * rows, blocks * edge))]
        + [sds((chips, nb, tok, edge), F32), sds((chips, nb, tok, edge))],
        [pltpu.VMEM((row_blocks, tok, edge), F32), pltpu.VMEM((blocks * edge, tok), BF16)],
        2,
        owner_section,
        output_lists,
        *parts,
        down_all,
        tout,
    )
    messages = gather(plain, wide)

    summed = keep + partner(send).astype(F32)
    total = summed[0]
    for c in range(1, chips):
        total = total + chip_swap(summed[c].astype(BF16), c).astype(F32)
    error = (total / zs).astype(BF16)
    near = spread(error)
    far = spread(shift(error, 2))

    (hidden_grad,) = call(
        functools.partial(back_kernel, **dims, slots=slots, blocks=blocks),
        [sds((tok, blocks * edge))],
        [pltpu.VMEM((row_blocks, tok, edge), BF16), pltpu.VMEM((tok, slots * edge), BF16)],
        1,
        output_lists,
        *near,
        down_all,
    )
    grads = [hidden_grad] + [shift(hidden_grad, s) for s in range(1, zs)]

    kept, passed = call(
        functools.partial(down_grad_kernel, **dims, **more),
        [sds(down_blocks.shape, F32), sds(down_blocks.shape)],
        [pltpu.VMEM((row_blocks, 2 * tok, edge), BF16), pltpu.VMEM((2 * rows, 2 * tok), BF16)],
        2,
        output_lists,
        output_counts,
        *near,
        *far,
        hidden_own,
        messages[1],
    )
    down_grad = (kept + shift(passed, 1).astype(F32)).astype(BF16)
    gate_grad, up_grad = call(
        functools.partial(up_grad_kernel, edge=edge, **more),
        [sds(gate_blocks.shape)] * 2,
        [pltpu.VMEM((zs * tok, 2 * edge), BF16)],
        1,
        input_counts,
        gathered,
        plain,
        *messages,
        *grads,
    )
    return gate_grad, up_grad, down_grad


def solution(mesh):
    weights = P("dp", None, "fsdp", None)
    rows = P("dp", "fsdp", None)

    def step(*args):
        block_rows, block_edge = args[3].shape[2:]
        if mesh.shape["fsdp"] != 4 or block_rows % 16 or args[0].shape[1] != block_edge:
            return plain_shards(*args)
        return shards(*args)

    return jax.shard_map(
        step,
        mesh=mesh,
        in_specs=(
            rows,
            rows,
            P("fsdp"),
            weights,
            weights,
            weights,
            P("dp", None),
            P("dp"),
            P("dp", None),
            P("dp"),
        ),
        out_specs=(weights, weights, weights),
        check_vma=False,
    )
```

```python
import functools

import jax
import jax.numpy as jnp
from jax import lax
from jax.experimental import pallas as pl
from jax.experimental.pallas import tpu as pltpu
from jax.sharding import PartitionSpec as P


F32 = jnp.float32
BF16 = jnp.bfloat16
VM = pl.BlockSpec(memory_space=pltpu.VMEM)
SM = pl.BlockSpec(memory_space=pltpu.SMEM)
TN = (((0,), (0,)), ((), ()))
NT = (((1,), (1,)), ((), ()))


def call(kernel, outs, scratch, smem, *args, space=VM):
    nbytes = sum(a.size * a.dtype.itemsize for a in args) + sum(
        o.size * o.dtype.itemsize for o in outs
    )
    return pl.pallas_call(
        kernel,
        out_shape=tuple(outs),
        in_specs=[SM] * smem + [space] * (len(args) - smem),
        out_specs=tuple(VM for _ in outs),
        scratch_shapes=scratch,
        compiler_params=pltpu.CompilerParams(vmem_limit_bytes=16 << 20),
        cost_estimate=pl.CostEstimate(flops=1 << 27, bytes_accessed=nbytes, transcendentals=0),
    )(*args)


def sds(shape, dtype=BF16):
    return jax.ShapeDtypeStruct(shape, dtype)


def far_end(z, zs):
    return jnp.logical_or(z == 0, z == zs - 1)


def turn_kernel(source, *refs, pieces, nb, edge):
    outs, tin, sems = refs[:2], refs[2], refs[3]
    d = lax.axis_index("dp")
    copies = []
    for r in range(pieces):
        at = pl.ds(pl.multiple_of(lax.bitwise_xor(d, r) * (nb * edge), edge), nb * edge)
        copies.append(pltpu.make_async_copy(source.at[:, at], tin.at[r], sems.at[r]))
    for r in list(range(1, pieces, 2)) + list(range(0, pieces, 2)):
        copies[r].start()
    for r in list(range(1, pieces, 2)) + list(range(0, pieces, 2)):
        copies[r].wait()
        for j in range(nb):
            lanes = slice(j * edge, (j + 1) * edge)
            outs[r % 2][r // 2, lanes, :] = tin[r, :, lanes].T


def relative_block(block, d, nb):
    return lax.bitwise_xor(block // nb, d) * nb + lax.rem(block, nb)


def pair_kernel(counts, gate, up, weights, *, rows, edge, slots, blocks):
    for f in range(blocks):
        count = counts[f]
        for k in range(slots):
            dst = slice(k * rows, (k + 1) * rows)
            live = k < count
            weights[f, dst, :edge] = jnp.where(live, gate[f, k], jnp.zeros_like(gate[f, k]))
            weights[f, dst, edge:] = jnp.where(live, up[f, k], jnp.zeros_like(up[f, k]))


def join_kernel(counts, *refs, zs, rows, edge, slots, blocks):
    downs, down_all = refs[: zs + 1], refs[zs + 1]
    z = lax.axis_index("fsdp")
    ends = far_end(z, zs)
    for f in range(blocks):
        count = counts[f]
        for k in range(slots):
            live = k < count
            for s in range(zs):
                at = pl.multiple_of(lax.bitwise_xor(z, s) * rows, rows)
                block = downs[s][f, k]
                if s == zs - 1:
                    block = jnp.where(ends, downs[zs][f, k], block)
                down_all[f, pl.ds(at, rows), k * edge : (k + 1) * edge] = jnp.where(
                    live, block, jnp.zeros_like(block)
                )


def partials(gathered, weights, outs, numbers, tok, edge, blocks):
    for f in range(blocks):
        lanes = slice(f * edge, (f + 1) * edge)
        for s, out in zip(numbers, outs):
            both = lax.dot_general(
                gathered[f, :, s * tok : (s + 1) * tok],
                weights[f],
                TN,
                preferred_element_type=F32,
            )
            out[0, :, lanes] = both[:, :edge].astype(out.dtype)
            out[1, :, lanes] = both[:, edge:].astype(out.dtype)


def front_kernel(lists, *refs, pieces, zs, nb, rows, edge, slots, blocks):
    xs = refs[:pieces]
    weights, last, gathered, xall = refs[pieces:]
    d = lax.axis_index("dp")
    tok = xs[0].shape[-1]
    for r in range(pieces):
        for s in range(zs):
            xall[r * nb * rows : (r + 1) * nb * rows, s * tok : (s + 1) * tok] = xs[r][s]
    for f in range(blocks):
        for k in range(slots):
            b = relative_block(lists[f, k], d, nb)
            dst = slice(k * rows, (k + 1) * rows)
            gathered[f, dst, :] = xall[pl.ds(pl.multiple_of(b * rows, rows), rows), :]
    partials(gathered, weights, [last], [zs - 1], tok, edge, blocks)


def rest_kernel(gathered, weights, *outs, edge, blocks):
    numbers = list(range(len(outs)))
    partials(gathered, weights, outs, numbers, outs[0].shape[1], edge, blocks)


def middle_kernel(
    owners, lists, *refs, pieces, zs, nb, rows, edge, slots, blocks
):
    parts = refs[:-9]
    down_all, tout, hidden_own, plain, wide, keep, send, acc, hidden_t = refs[-9:]
    d, z, owner = lax.axis_index("dp"), lax.axis_index("fsdp"), owners[0]
    tok = tout.shape[0]
    own = owner == d
    for b in range(pieces * nb):
        term = tout[:, b * edge : (b + 1) * edge].astype(F32)
        acc[b] = jnp.where(own, -term, jnp.zeros_like(term))
    for f in range(blocks):
        lanes = slice(f * edge, (f + 1) * edge)
        g = parts[0][0, :, lanes].astype(F32)
        u = parts[0][1, :, lanes].astype(F32)
        for part in parts[1:]:
            g += part[0, :, lanes].astype(F32)
            u += part[1, :, lanes].astype(F32)
        sig = jax.nn.sigmoid(g)
        act = g * sig
        hidden = (act * u).astype(BF16)
        slope = (u * sig * (1.0 + g * (1.0 - sig))).astype(BF16)
        for message in (plain, wide):
            message[:tok, lanes] = slope
            message[tok : 2 * tok, lanes] = act.astype(BF16)
        hidden_t[lanes, :] = hidden.T
        prod = jnp.dot(hidden, down_all[f], preferred_element_type=F32)
        for k in range(slots):
            acc[lists[f, k]] += prod[:, k * edge : (k + 1) * edge]
        for s in range(zs):
            at = pl.multiple_of(f * edge + lax.bitwise_xor(z, s) * rows, rows)
            cut = hidden_t[pl.ds(at, rows), :]
            slot = slice(2 * tok + s % 2 * rows, 2 * tok + (s % 2 + 1) * rows)
            if s < 2:
                hidden_own[s, f * rows : (f + 1) * rows, :] = cut
            else:
                wide[slot, lanes] = cut
    for r in range(pieces):
        for j in range(nb):
            value = acc[lax.bitwise_xor(d, r) * nb + j]
            if r % 2:
                send[r // 2, j] = value.astype(BF16)
            else:
                keep[r // 2, j] = value


def back_kernel(lists, *refs, pieces, nb, edge, slots, blocks):
    es = refs[:pieces]
    down_all, out, eall, ecat = refs[pieces:]
    d = lax.axis_index("dp")
    for r in range(pieces):
        eall[r * nb : (r + 1) * nb] = es[r][...]
    for f in range(blocks):
        for k in range(slots):
            ecat[:, k * edge : (k + 1) * edge] = eall[relative_block(lists[f, k], d, nb)]
        out[:, f * edge : (f + 1) * edge] = lax.dot_general(
            ecat[...], down_all[f], NT, preferred_element_type=F32
        ).astype(BF16)


def down_grad_kernel(lists, counts, *refs, pieces, zs, nb, rows, edge, slots, blocks):
    own = refs[:pieces]
    far = refs[pieces : 2 * pieces]
    hidden_own, message = refs[2 * pieces : 2 * pieces + 2]
    keep, send, eall, hid = refs[2 * pieces + 2 :]
    d = lax.axis_index("dp")
    tok = hidden_own.shape[-1]
    for r in range(pieces):
        for j in range(nb):
            eall[r * nb + j, :tok, :] = own[r][j]
            eall[r * nb + j, tok:, :] = far[r][j]
    for f in range(blocks):
        lanes = slice(f * edge, (f + 1) * edge)
        for side in range(2):
            dst = slice(side * rows, (side + 1) * rows)
            hid[dst, :tok] = hidden_own[side, f * rows : (f + 1) * rows, :]
            hid[dst, tok:] = message[2 * tok + side * rows : 2 * tok + (side + 1) * rows, lanes]
        count = counts[f]
        for k in range(slots):
            grad = jnp.dot(
                hid[...],
                eall[relative_block(lists[f, k], d, nb)],
                preferred_element_type=F32,
            )
            grad = jnp.where(k < count, grad, jnp.zeros_like(grad))
            keep[f, k] = grad[:rows]
            send[f, k] = grad[rows:].astype(BF16)


def up_grad_kernel(counts, *refs, zs, rows, edge, slots, blocks):
    gathered = refs[0]
    factors = refs[1 : 2 + zs]
    errors = refs[2 + zs : 2 + 2 * zs]
    gate_out, up_out, both = refs[2 + 2 * zs :]
    tok = errors[0].shape[0]
    ends = far_end(lax.axis_index("fsdp"), zs)
    for f in range(blocks):
        count = counts[f]
        lanes = slice(f * edge, (f + 1) * edge)
        for s in range(zs):
            dh = errors[s][:, lanes].astype(F32)
            at = slice(s * tok, (s + 1) * tok)
            for side in range(2):
                span = slice(side * tok, (side + 1) * tok)
                factor = factors[s][span, lanes]
                if s == zs - 1:
                    factor = jnp.where(ends, factors[zs][span, lanes], factor)
                both[at, side * edge : (side + 1) * edge] = (dh * factor.astype(F32)).astype(BF16)
        grad = jnp.dot(gathered[f], both[...], preferred_element_type=F32)
        for k in range(slots):
            part = grad[k * rows : (k + 1) * rows]
            part = jnp.where(k < count, part, jnp.zeros_like(part)).astype(BF16)
            gate_out[f, k] = part[:, :edge]
            up_out[f, k] = part[:, edge:]


def broadcast(shard, axis, root):
    mine = lax.axis_index(axis) == root
    return lax.psum(jnp.where(mine, shard, jnp.zeros_like(shard)), axis)


def live_mask(counts, slot_count):
    positions = jnp.arange(slot_count, dtype=jnp.int32)
    return (positions[None, :] < counts[:, None])[:, :, None, None]


def plain_shards(
    teacher_in,
    teacher_out,
    owner_section,
    gate_blocks,
    up_blocks,
    down_blocks,
    input_lists,
    input_counts,
    output_lists,
    output_counts,
):
    root_section = owner_section[0]
    local_in = teacher_in[0]
    local_out = teacher_out[0]
    micro_count = lax.axis_size("fsdp")
    rows_in = broadcast(local_in, "dp", root_section)
    gate_full, up_full, down_full = (
        lax.all_gather(gate_blocks, "fsdp", axis=2, tiled=True),
        lax.all_gather(up_blocks, "fsdp", axis=2, tiled=True),
        lax.all_gather(down_blocks, "fsdp", axis=2, tiled=True),
    )
    slot_count = input_lists.shape[1]
    block_edge = gate_full.shape[3]
    tok_rows = rows_in.shape[0]
    model_width = rows_in.shape[1]
    row_blocks = model_width // block_edge
    input_live = live_mask(input_counts, slot_count)
    output_live = live_mask(output_counts, slot_count)
    zero_value = jnp.zeros((), jnp.bfloat16)
    gate_live = jnp.where(input_live, gate_full, zero_value)
    up_live = jnp.where(input_live, up_full, zero_value)
    down_live = jnp.where(output_live, down_full, zero_value)
    picked = rows_in.reshape(tok_rows, row_blocks, block_edge)[:, input_lists]
    gate_pre = jnp.einsum("tfki,fkio->tfo", picked, gate_live, preferred_element_type=jnp.float32)
    up_pre = jnp.einsum("tfki,fkio->tfo", picked, up_live, preferred_element_type=jnp.float32)
    sigmoid_gate = jax.nn.sigmoid(gate_pre)
    activated = gate_pre * sigmoid_gate
    hidden = (activated * up_pre).astype(jnp.bfloat16)
    pieces = jnp.einsum("tfi,fkio->tfko", hidden, down_live, preferred_element_type=jnp.float32)
    blank_out = jnp.zeros((tok_rows, row_blocks, block_edge), jnp.float32)
    partial_out = blank_out.at[:, output_lists].add(pieces).reshape(tok_rows, model_width)
    is_owner = lax.axis_index("dp") == root_section
    own_term = jnp.where(is_owner, local_out.astype(jnp.float32), jnp.float32(0.0))
    residual_rows = lax.psum((partial_out - own_term).astype(jnp.bfloat16), "dp").astype(
        jnp.float32
    )
    scaled_error = (residual_rows / micro_count).astype(jnp.bfloat16)
    error_picked = scaled_error.reshape(tok_rows, row_blocks, block_edge)[:, output_lists]
    output_scale = output_live.astype(jnp.float32)
    input_scale = input_live.astype(jnp.float32)
    down_grad = (
        jnp.einsum("tfi,tfko->fkio", hidden, error_picked, preferred_element_type=jnp.float32)
        * output_scale
    )
    hidden_grad = jnp.einsum(
        "tfko,fkio->tfi", error_picked, down_live, preferred_element_type=jnp.float32
    )
    gate_error = (
        hidden_grad * up_pre * sigmoid_gate * (1.0 + gate_pre * (1.0 - sigmoid_gate))
    ).astype(jnp.bfloat16)
    up_error = (hidden_grad * activated).astype(jnp.bfloat16)
    gate_grad = (
        jnp.einsum("tfki,tfo->fkio", picked, gate_error, preferred_element_type=jnp.float32)
        * input_scale
    )
    up_grad = (
        jnp.einsum("tfki,tfo->fkio", picked, up_error, preferred_element_type=jnp.float32)
        * input_scale
    )
    gate_sum, up_sum, down_sum = (
        lax.psum_scatter(
            gate_grad.astype(jnp.bfloat16), "fsdp", scatter_dimension=2, tiled=True
        ).astype(jnp.float32),
        lax.psum_scatter(
            up_grad.astype(jnp.bfloat16), "fsdp", scatter_dimension=2, tiled=True
        ).astype(jnp.float32),
        lax.psum_scatter(
            down_grad.astype(jnp.bfloat16), "fsdp", scatter_dimension=2, tiled=True
        ).astype(jnp.float32),
    )
    return (
        gate_sum.astype(jnp.bfloat16),
        up_sum.astype(jnp.bfloat16),
        down_sum.astype(jnp.bfloat16),
    )


def shards(
    teacher_in,
    teacher_out,
    owner_section,
    gate_blocks,
    up_blocks,
    down_blocks,
    input_lists,
    input_counts,
    output_lists,
    output_counts,
):
    pieces, zs = lax.axis_size("dp"), lax.axis_size("fsdp")
    d, z = lax.axis_index("dp"), lax.axis_index("fsdp")
    owner = owner_section[0]
    tin, tout = teacher_in[0], teacher_out[0]
    blocks, slots, rows, edge = gate_blocks.shape
    tok, width = tin.shape
    row_blocks = width // edge
    nb = row_blocks // pieces
    chips = pieces // 2
    dims = dict(pieces=pieces, nb=nb, edge=edge)
    more = dict(zs=zs, rows=rows, slots=slots, blocks=blocks)

    def partner(a):
        return lax.ppermute(a, "dp", [(i, i ^ 1) for i in range(pieces)])

    def chip_swap(a, c):
        return lax.ppermute(a, "dp", [(i, i ^ (2 * c)) for i in range(pieces)])

    def shift(a, s):
        return lax.ppermute(a, "fsdp", [(i, i ^ s) for i in range(zs)])

    def move(a, pairs):
        return lax.ppermute(a, "fsdp", pairs)

    def gather(plain, wide):
        side = shift(plain, 1)
        cross = shift(wide, 2)
        inner = move(plain, [(1, 2), (2, 1)])
        core = cross[: plain.shape[0]]
        return [side, cross, inner, move(core, [(1, 0), (2, 3)])]

    def collect(mine):
        joined = move(mine[3], [(0, 1), (3, 2)])
        cross = move(mine[2], [(0, 2), (3, 1)])
        inner = move(mine[3], [(1, 2), (2, 1)])
        pair = shift(mine[1], 1)
        both = (mine[2].astype(F32) + joined.astype(F32)).astype(BF16)
        return [mine[0], pair, cross, inner, move(both, [(2, 0), (1, 3)])]

    def spread(a):
        per_chip = [a] + [chip_swap(a, c) for c in range(1, chips)]
        out = []
        for p in per_chip:
            out += [p, partner(p)]
        return out

    downs = [down_blocks] + gather(down_blocks, down_blocks)

    half = sds((chips, nb * edge, tok))
    kept, sent = call(
        functools.partial(turn_kernel, **dims),
        [half, half],
        [pltpu.VMEM((pieces, tok, nb * edge), BF16), pltpu.SemaphoreType.DMA((pieces,))],
        0,
        tin,
        space=pl.BlockSpec(memory_space=pl.ANY),
    )
    met = partner(sent)
    is_owner = owner == d
    own_chip = lax.bitwise_xor(owner // 2, d // 2)
    piece = jnp.where(is_owner, kept[0], met[0])
    for c in range(1, chips):
        got = chip_swap(jnp.where(is_owner, kept[c], met[c]), c)
        piece = jnp.where(own_chip == c, got, piece)
    piece = piece.reshape(nb, zs, rows, tok)
    cut = [
        lax.dynamic_index_in_dim(piece, lax.bitwise_xor(z, s), 1, keepdims=False)
        for s in range(zs)
    ]
    mixed = jnp.stack([cut[0]] + [shift(cut[s], s) for s in range(1, zs)])
    xs = spread(mixed.reshape(zs, nb * rows, tok))

    part = sds((2, tok, blocks * edge))
    inner_sizes = dict(rows=rows, edge=edge, slots=slots, blocks=blocks)
    (weights,) = call(
        functools.partial(pair_kernel, **inner_sizes),
        [sds((blocks, slots * rows, 2 * edge))],
        [],
        1,
        input_counts,
        gate_blocks,
        up_blocks,
    )
    last, gathered = call(
        functools.partial(front_kernel, **dims, **more),
        [part, sds((blocks, slots * rows, zs * tok))],
        [pltpu.VMEM((row_blocks * rows, zs * tok), BF16)],
        1,
        input_lists,
        *xs,
        weights,
    )
    rest = call(
        functools.partial(rest_kernel, edge=edge, blocks=blocks),
        [sds(part.shape, F32)] + [part] * (zs - 2),
        [],
        0,
        gathered,
        weights,
    )
    parts = collect([*rest, last])

    (down_all,) = call(
        functools.partial(join_kernel, zs=zs, **inner_sizes),
        [sds((blocks, edge, slots * edge))],
        [],
        1,
        output_counts,
        *downs,
    )
    hidden_own, plain, wide, keep, send = call(
        functools.partial(middle_kernel, **dims, **more),
        [sds((2, blocks * rows, tok)), sds((2 * tok, blocks * edge))]
        + [sds((2 * tok + 2 * rows, blocks * edge))]
        + [sds((chips, nb, tok, edge), F32), sds((chips, nb, tok, edge))],
        [pltpu.VMEM((row_blocks, tok, edge), F32), pltpu.VMEM((blocks * edge, tok), BF16)],
        2,
        owner_section,
        output_lists,
        *parts,
        down_all,
        tout,
    )
    messages = gather(plain, wide)

    summed = keep + partner(send).astype(F32)
    total = summed[0]
    for c in range(1, chips):
        total = total + chip_swap(summed[c].astype(BF16), c).astype(F32)
    error = (total / zs).astype(BF16)
    near = spread(error)
    far = spread(shift(error, 2))

    (hidden_grad,) = call(
        functools.partial(back_kernel, **dims, slots=slots, blocks=blocks),
        [sds((tok, blocks * edge))],
        [pltpu.VMEM((row_blocks, tok, edge), BF16), pltpu.VMEM((tok, slots * edge), BF16)],
        1,
        output_lists,
        *near,
        down_all,
    )
    grads = [hidden_grad] + [shift(hidden_grad, s) for s in range(1, zs)]

    kept, passed = call(
        functools.partial(down_grad_kernel, **dims, **more),
        [sds(down_blocks.shape, F32), sds(down_blocks.shape)],
        [pltpu.VMEM((row_blocks, 2 * tok, edge), BF16), pltpu.VMEM((2 * rows, 2 * tok), BF16)],
        2,
        output_lists,
        output_counts,
        *near,
        *far,
        hidden_own,
        messages[1],
    )
    down_grad = (kept + shift(passed, 1).astype(F32)).astype(BF16)
    gate_grad, up_grad = call(
        functools.partial(up_grad_kernel, edge=edge, **more),
        [sds(gate_blocks.shape)] * 2,
        [pltpu.VMEM((zs * tok, 2 * edge), BF16)],
        1,
        input_counts,
        gathered,
        plain,
        *messages,
        *grads,
    )
    return gate_grad, up_grad, down_grad


def solution(mesh):
    weights = P("dp", None, "fsdp", None)
    rows = P("dp", "fsdp", None)

    def step(*args):
        block_rows, block_edge = args[3].shape[2:]
        if mesh.shape["fsdp"] != 4 or block_rows % 16 or args[0].shape[1] != block_edge:
            return plain_shards(*args)
        return shards(*args)

    return jax.shard_map(
        step,
        mesh=mesh,
        in_specs=(
            rows,
            rows,
            P("fsdp"),
            weights,
            weights,
            weights,
            P("dp", None),
            P("dp"),
            P("dp", None),
            P("dp"),
        ),
        out_specs=(weights, weights, weights),
        check_vma=False,
    )
```
